128 devices in a mesh: row: 8 (over y, x_lo), col: 16 (over z, x_hi, core).
Axes of the slice: x: 4 (x_hi: 2, x_lo: 2; x = x_hi * 2 + x_lo), y: 4, z: 4, core: 2. Of those that a mesh axis runs over, the one named last changes fastest.
Arguments:
- pair: bfloat16 [256, 256, 128], P('row', 'col'), may hold values from -6 to 6
- cotangent: bfloat16 [256, 256, 128], P('row', 'col'), may hold values from -6 to 6
- token_mask: int32 [256], replicated, may hold values 0 or 1
- out_in_proj: bfloat16 [128, 640], replicated, may hold values from -0.5 to 0.5
- out_out_proj: bfloat16 [128, 128], replicated, may hold values from -0.5 to 0.5
- in_in_proj: bfloat16 [128, 640], replicated, may hold values from -0.5 to 0.5
- in_out_proj: bfloat16 [128, 128], replicated, may hold values from -0.5 to 0.5
Outputs:
- updated_pair: bfloat16 [256, 256, 128], P('row', 'col')
- pair_grad: bfloat16 [256, 256, 128], P('row', 'col')
- out_in_grad: float32 [128, 640], replicated
- out_out_grad: float32 [128, 128], replicated
- in_in_grad: float32 [128, 640], replicated
- in_out_grad: float32 [128, 128], replicated
The draws below stay inside these ranges and needn't reach their ends.
All inputs are finite; a program needn't handle non-finite values.
Results may differ from the reference program's by a relative error of at most 0.012.
Values may be sent and summed in bfloat16 or wider, within the bound.
A program may use at most 128 MiB of HBM per device.

```python
import jax
import jax.numpy as jnp
from jax import lax

C = 128
H = 128
TOKENS = 256


def with_ends(values, stream_key, low, largest):
    longest = values.shape.index(max(values.shape))
    spots = []
    for shift in (0, 1):
        where = [jax.random.randint(jax.random.fold_in(stream_key, axis), (), 0, length) for axis, length in enumerate(values.shape)]
        where[longest] = (where[longest] + shift) % values.shape[longest]
        spots.append(tuple(where))
    return values.at[spots[0]].set(low).at[spots[1]].set(largest)


def shard_levels(own_key, extent, split, least, largest):
    gain, own = 1.0, jax.random.fold_in(own_key, 6)
    for axis_at, blocks in split:
        heights = jnp.exp(jax.random.uniform(jax.random.fold_in(own, axis_at), (blocks,), jnp.float32, least / len(split), largest / len(split)))
        gain = gain * jnp.repeat(heights, extent[axis_at] // blocks).reshape([-1 if axis == axis_at else 1 for axis in range(len(extent))])
    return gain


def centred(rng, extent, scale, reach, shards=(), kind=jnp.bfloat16):
    loudness = shard_levels(rng, extent, shards, -0.22, 0.18) if shards else 1.0
    entries = jax.random.normal(rng, extent, jnp.float32) * scale * loudness
    return jnp.minimum(jnp.maximum(entries, -reach), reach).astype(kind)


def setup_inputs(seed: int = 0) -> dict:
    streams_of = jax.random.split(jax.random.key(seed), 8)
    return {
        "pair": centred(streams_of[0], (TOKENS, TOKENS, C), 1.0, 6.0, ((0, 8), (1, 16))),
        "cotangent": centred(streams_of[1], (TOKENS, TOKENS, C), 1.0, 6.0, ((0, 8), (1, 16))),
        "token_mask": with_ends((jax.random.randint(streams_of[2], (TOKENS,), 0, 8) < 7).astype(jnp.int32), jax.random.fold_in(streams_of[2], 1), 0, 1),
        "out_in_proj": centred(streams_of[3], (C, 4 * H + C), C ** -0.5, 0.5),
        "out_out_proj": centred(streams_of[4], (H, C), H ** -0.5, 0.5),
        "in_in_proj": centred(streams_of[5], (C, 4 * H + C), C ** -0.5, 0.5),
        "in_out_proj": centred(streams_of[6], (H, C), H ** -0.5, 0.5),
    }


EPSILON = 1e-05

def normalize(values):
    centre = lax.optimization_barrier(jnp.mean(values, axis=-1, keepdims=True))
    shifted = values - centre
    spread = lax.optimization_barrier(jnp.mean(shifted * shifted, axis=-1, keepdims=True))
    return shifted * lax.rsqrt(spread + EPSILON)

def gating(projected, pair_mask):
    left_value = projected[..., :H]
    left_gate = projected[..., H:2 * H]
    right_value = projected[..., 2 * H:3 * H]
    right_gate = projected[..., 3 * H:4 * H]
    left_full = jax.nn.sigmoid(left_gate) * left_value * pair_mask
    right_full = jax.nn.sigmoid(right_gate) * right_value * pair_mask
    return (left_full, right_full, jax.nn.sigmoid(projected[..., 4 * H:]))

def triangle(left_tile, right_tile, outgoing):
    left_wide = left_tile.astype(jnp.float32)
    right_wide = right_tile.astype(jnp.float32)
    if outgoing:
        return jnp.einsum('ikh,jkh->ijh', left_wide, right_wide)
    return jnp.einsum('kih,kjh->ijh', left_wide, right_wide)

def triangle_grads(tri_grad, left_tile, right_tile, outgoing):
    grad_wide = tri_grad.astype(jnp.float32)
    left_wide = left_tile.astype(jnp.float32)
    right_wide = right_tile.astype(jnp.float32)
    if outgoing:
        left_grad = jnp.einsum('ijh,jkh->ikh', grad_wide, right_wide)
        right_grad = jnp.einsum('ijh,ikh->jkh', grad_wide, left_wide)
    else:
        left_grad = jnp.einsum('ijh,kjh->kih', grad_wide, right_wide)
        right_grad = jnp.einsum('ijh,kih->kjh', grad_wide, left_wide)
    return (left_grad, right_grad)

def forward(pair_in, pair_mask, w_in, w_out, outgoing):
    pair_wide = pair_in.astype(jnp.float32)
    normed = normalize(pair_wide).astype(jnp.bfloat16)
    projected = jnp.dot(normed, w_in, preferred_element_type=jnp.float32)
    left_full, right_full, gate = gating(projected, pair_mask)
    left_tile = left_full.astype(jnp.bfloat16)
    right_tile = right_full.astype(jnp.bfloat16)
    triangle_sum = triangle(left_tile, right_tile, outgoing)
    tri_normed = normalize(triangle_sum).astype(jnp.bfloat16)
    lifted = jnp.dot(tri_normed, w_out, preferred_element_type=jnp.float32)
    result = (pair_wide + gate * lifted).astype(jnp.bfloat16)
    saved = (pair_wide, normed, projected, left_tile, right_tile, gate, triangle_sum, tri_normed, lifted)
    return (result, saved)

def backward(cotan, saved, pair_mask, w_in, w_out, outgoing):
    pair_wide, normed, projected, left_tile, right_tile, gate, triangle_sum, tri_normed, lifted = saved
    cot_wide = cotan.astype(jnp.float32)
    lift_grad = gate * cot_wide
    gate_grad = lifted * cot_wide
    out_grad = jnp.einsum('ijh,ijc->hc', tri_normed.astype(jnp.float32), lift_grad, precision=lax.Precision.HIGHEST)
    normed_tri_grad = jnp.dot(lift_grad, w_out.astype(jnp.float32).T, precision=lax.Precision.HIGHEST)
    tri_grad = jax.vjp(normalize, triangle_sum)[1](normed_tri_grad)[0].astype(jnp.bfloat16)
    left_grad, right_grad = triangle_grads(tri_grad, left_tile, right_tile, outgoing)
    gate_vjp = jax.vjp(lambda values: gating(values, pair_mask), projected)[1]
    proj_grad = gate_vjp((left_grad, right_grad, gate_grad))[0]
    in_grad = jnp.einsum('ijc,ijq->cq', normed.astype(jnp.float32), proj_grad, precision=lax.Precision.HIGHEST)
    normed_grad = jnp.dot(proj_grad, w_in.astype(jnp.float32).T, precision=lax.Precision.HIGHEST)
    pair_grad = (cot_wide + jax.vjp(normalize, pair_wide)[1](normed_grad)[0]).astype(jnp.bfloat16)
    return (pair_grad, in_grad, out_grad)

def reference(pair, cotangent, token_mask, out_in_proj, out_out_proj, in_in_proj, in_out_proj):
    flags = token_mask.astype(jnp.float32)
    pair_mask = (flags[:, None] * flags[None, :])[:, :, None]
    middle, saved_out = forward(pair, pair_mask, out_in_proj, out_out_proj, True)
    updated, saved_in = forward(middle, pair_mask, in_in_proj, in_out_proj, False)
    middle_grad, in_in_grad, in_out_grad = backward(cotangent, saved_in, pair_mask, in_in_proj, in_out_proj, False)
    pair_grad, out_in_grad, out_out_grad = backward(middle_grad, saved_out, pair_mask, out_in_proj, out_out_proj, True)
    return (updated, pair_grad, out_in_grad / TOKENS, out_out_grad / TOKENS, in_in_grad / TOKENS, in_out_grad / TOKENS)
```

```python
import jax
import jax.numpy as jnp
from jax import lax
from jax.experimental import pallas as pl
from jax.experimental.pallas import tpu as pltpu
from jax.sharding import PartitionSpec as P

MESH = pl.DeviceIdType.MESH
N = 128

H = 128


EPSILON = 1e-05


def shortened(array):
    return jax.tree.map(lambda a: a.astype(jnp.bfloat16) if a.dtype == jnp.float32 else a, array)


def from_everyone(array, axis):
    copies = jnp.broadcast_to(array, (lax.axis_size(axis), *array.shape))
    return lax.all_to_all(copies, axis, split_axis=0, concat_axis=0, tiled=True)


def in_order(tiles, dim):
    shape = list(tiles.shape[1:])
    shape[dim] *= tiles.shape[0]
    return jnp.moveaxis(tiles, 0, dim).reshape(shape)


def collect(array, axis, dim):
    tiles = from_everyone(array, axis)
    return in_order(tiles, dim)


def normalize(values):
    centre = jnp.mean(values, axis=-1, keepdims=True)
    shifted = values - centre
    spread = jnp.mean(shifted * shifted, axis=-1, keepdims=True)
    return shifted * lax.rsqrt(spread + EPSILON)


def gating(projected, pair_mask):
    left_value = projected[..., :H]
    left_gate = projected[..., H : 2 * H]
    right_value = projected[..., 2 * H : 3 * H]
    right_gate = projected[..., 3 * H : 4 * H]
    left_full = jax.nn.sigmoid(left_gate) * left_value * pair_mask
    right_full = jax.nn.sigmoid(right_gate) * right_value * pair_mask
    return (left_full, right_full, jax.nn.sigmoid(projected[..., 4 * H :]))


def cols_of(tiles):
    return jax.tree.map(
        lambda part, own: part.astype(own.dtype),
        lax.all_gather(shortened(tiles), "col", axis=1, tiled=True),
        tiles,
    )


def rows_of(tiles):
    return jax.tree.map(
        lambda part, own: part.astype(own.dtype),
        jax.tree.map(lambda part: collect(part, "row", 0), shortened(tiles)),
        tiles,
    )


def to_row_blocks(panel):
    return lax.all_to_all(panel, "col", split_axis=0, concat_axis=1, tiled=True)


def to_col_blocks(panel):
    return lax.all_to_all(panel, "row", split_axis=1, concat_axis=0, tiled=True)


def outgoing_sum(left_tile, right_tile):
    row_panels = rows_of((left_tile, right_tile))
    left_panel = cols_of(left_tile)
    right_rows = to_row_blocks(row_panels[1])
    total = jnp.einsum("ikh,jkh->ijh", left_panel, right_rows, preferred_element_type=jnp.float32)
    return (total, row_panels)


def incoming_sum(left_tile, right_tile):
    col_panels = cols_of((left_tile, right_tile))
    right_all = rows_of(right_tile)
    left_cols = to_col_blocks(col_panels[0])
    total = jnp.einsum("kih,kjh->ijh", left_cols, right_all, preferred_element_type=jnp.float32)
    return (total, col_panels)


def outgoing_grads(tri_grad, row_panels):
    grad_cols = cols_of(tri_grad)
    grad_rows = to_col_blocks(grad_cols)
    left_grad = jnp.einsum(
        "ijh,jkh->ikh", grad_cols, row_panels[1], preferred_element_type=jnp.float32
    )
    right_grad = jnp.einsum(
        "ijh,ikh->jkh", grad_rows, row_panels[0], preferred_element_type=jnp.float32
    )
    return (left_grad, right_grad)


def incoming_grads(tri_grad, col_panels):
    grad_rows = rows_of(tri_grad)
    grad_cols = to_row_blocks(grad_rows)
    left_grad = jnp.einsum(
        "ijh,kjh->kih", grad_cols, col_panels[1], preferred_element_type=jnp.float32
    )
    right_grad = jnp.einsum(
        "kih,ijh->kjh", col_panels[0], grad_rows, preferred_element_type=jnp.float32
    )
    return (left_grad, right_grad)


def forward(pair_in, pair_mask, w_in, w_out, outgoing):
    pair_wide = pair_in.astype(jnp.float32)
    normed = normalize(pair_wide).astype(jnp.bfloat16)
    projected = jnp.dot(normed, w_in, preferred_element_type=jnp.float32)
    left_full, right_full, gate = gating(projected, pair_mask)
    left_tile = left_full.astype(jnp.bfloat16)
    right_tile = right_full.astype(jnp.bfloat16)
    if outgoing:
        triangle_sum, panels = outgoing_sum(left_tile, right_tile)
    else:
        triangle_sum, panels = incoming_sum(left_tile, right_tile)
    tri_normed = normalize(triangle_sum).astype(jnp.bfloat16)
    lifted = jnp.dot(tri_normed, w_out, preferred_element_type=jnp.float32)
    result = (pair_wide + gate * lifted).astype(jnp.bfloat16)
    saved = (pair_wide, normed, projected, gate, triangle_sum, tri_normed, lifted, panels)
    return (result, saved)


def backward(cotan, saved, pair_mask, w_in, w_out, outgoing):
    pair_wide, normed, projected, gate, triangle_sum, tri_normed, lifted, panels = saved
    cot_wide = cotan.astype(jnp.float32)
    lift_grad = gate * cot_wide
    gate_grad = lifted * cot_wide
    out_grad = jnp.einsum(
        "ijh,ijc->hc", tri_normed.astype(jnp.float32), lift_grad, precision=lax.Precision.HIGHEST
    )
    normed_tri_grad = jnp.dot(
        lift_grad, w_out.astype(jnp.float32).T, precision=lax.Precision.HIGHEST
    )
    tri_grad = jax.vjp(normalize, triangle_sum)[1](normed_tri_grad)[0].astype(jnp.bfloat16)
    if outgoing:
        left_grad, right_grad = outgoing_grads(tri_grad, panels)
    else:
        left_grad, right_grad = incoming_grads(tri_grad, panels)
    gate_vjp = jax.vjp(lambda values: gating(values, pair_mask), projected)[1]
    proj_grad = gate_vjp((left_grad, right_grad, gate_grad))[0]
    in_grad = jnp.einsum(
        "ijc,ijq->cq", normed.astype(jnp.float32), proj_grad, precision=lax.Precision.HIGHEST
    )
    normed_grad = jnp.dot(proj_grad, w_in.astype(jnp.float32).T, precision=lax.Precision.HIGHEST)
    pair_grad = (cot_wide + jax.vjp(normalize, pair_wide)[1](normed_grad)[0]).astype(jnp.bfloat16)
    return (pair_grad, in_grad, out_grad)


def reduce_kernel(x_ref, o_ref, got, total, ssem, rsem):
    cols = lax.axis_size("col")
    me = lax.axis_index("row") * cols + lax.axis_index("col")

    def peer(step):
        other = lax.rem(me + step, N)
        return (other // cols, lax.rem(other, cols))

    bar = pltpu.get_barrier_semaphore()

    @pl.loop(1, N)
    def _(step):
        pl.semaphore_signal(bar, inc=1, device_id=peer(step), device_id_type=MESH)

    pl.semaphore_wait(bar, N - 1)

    def await_all(ref, sem):
        part = ref.at[pl.ds(0, N - 1)]
        pltpu.make_async_copy(part, part, sem).wait()

    @pl.loop(1, N)
    def _(step):
        a, b = peer(step)
        pltpu.make_async_remote_copy(
            src_ref=x_ref.at[a * cols + b], dst_ref=got.at[me], send_sem=ssem.at[0],
            recv_sem=rsem.at[0], device_id=(a, b), device_id_type=MESH,
        ).start()

    got[me] = x_ref[me]
    await_all(got, rsem.at[0])
    total[...] = jnp.sum(got[...].astype(jnp.float32), axis=0).astype(jnp.bfloat16)

    @pl.loop(1, N)
    def _(step):
        pltpu.make_async_remote_copy(
            src_ref=total, dst_ref=o_ref.at[me], send_sem=ssem.at[1],
            recv_sem=rsem.at[1], device_id=peer(step), device_id_type=MESH,
        ).start()

    o_ref[me] = total[...]
    await_all(got, ssem.at[0])
    await_all(o_ref, rsem.at[1])
    await_all(o_ref, ssem.at[1])


def reduce_all(parts):
    flat = jnp.concatenate([part.reshape(-1, 128) for part in parts], axis=0)
    tiles = flat.reshape(N, -1, 128)
    rows = tiles.shape[1]
    tiles = jnp.pad(tiles, ((0, 0), (0, 16 - rows), (0, 0))).astype(jnp.bfloat16)
    out = pl.pallas_call(
        reduce_kernel,
        out_shape=jax.ShapeDtypeStruct(tiles.shape, jnp.bfloat16),
        in_specs=[pl.BlockSpec(memory_space=pltpu.VMEM)],
        out_specs=pl.BlockSpec(memory_space=pltpu.VMEM),
        scratch_shapes=[
            pltpu.VMEM(tiles.shape, jnp.bfloat16),
            pltpu.VMEM(tiles.shape[1:], jnp.bfloat16),
            pltpu.SemaphoreType.DMA((2,)),
            pltpu.SemaphoreType.DMA((2,)),
        ],
        compiler_params=pltpu.CompilerParams(collective_id=0, has_side_effects=True),
    )(tiles)
    flat = out[:, :rows].astype(jnp.float32).reshape(-1, 128)
    totals, at = [], 0
    for part in parts:
        size = part.size // 128
        totals.append(flat[at : at + size].reshape(part.shape))
        at += size
    return totals


def local(pair, cotangent, token_mask, out_in_proj, out_out_proj, in_in_proj, in_out_proj):
    row_tile = pair.shape[0]
    col_tile = pair.shape[1]
    row_flags = lax.dynamic_slice_in_dim(
        token_mask, lax.axis_index("row") * row_tile, row_tile, 0
    ).astype(jnp.float32)
    col_flags = lax.dynamic_slice_in_dim(
        token_mask, lax.axis_index("col") * col_tile, col_tile, 0
    ).astype(jnp.float32)
    pair_mask = (row_flags[:, None] * col_flags[None, :])[:, :, None]
    middle, saved_out = forward(pair, pair_mask, out_in_proj, out_out_proj, True)
    updated, saved_in = forward(middle, pair_mask, in_in_proj, in_out_proj, False)
    middle_grad, in_in_part, in_out_part = backward(
        cotangent, saved_in, pair_mask, in_in_proj, in_out_proj, False
    )
    pair_grad, out_in_part, out_out_part = backward(
        middle_grad, saved_out, pair_mask, out_in_proj, out_out_proj, True
    )
    totals = reduce_all((out_in_part, out_out_part, in_in_part, in_out_part))
    tokens_all = row_tile * lax.axis_size("row")
    return (
        updated,
        pair_grad,
        totals[0] / tokens_all,
        totals[1] / tokens_all,
        totals[2] / tokens_all,
        totals[3] / tokens_all,
    )


def solution(mesh):
    return jax.shard_map(
        local,
        mesh=mesh,
        in_specs=(P("row", "col", None), P("row", "col", None), P(), P(), P(), P(), P()),
        out_specs=(P("row", "col", None), P("row", "col", None), P(), P(), P(), P()),
        check_vma=False,
    )
```

```python
import jax
import jax.numpy as jnp
from jax import lax
from jax.experimental import pallas as pl
from jax.experimental.pallas import tpu as pltpu
from jax.sharding import PartitionSpec as P

MESH = pl.DeviceIdType.MESH
F32 = jnp.float32
BF16 = jnp.bfloat16
EPSILON = 1e-05
N = 128
H = 128
ROWS, COLS = 32, 16
CHUNKS = 4
TOKENS = 256
OUT_LR, OUT_TRI, IN_LR, IN_TRI, IN_BACK, IN_SIDES, OUT_BACK, OUT_SIDES = range(8)
IN_SUM, IN_SHARE, OUT_SUM, OUT_SHARE = range(8, 12)
EXCHANGES = 12


def nn(a, b):
    return lax.dot_general(a, b, (((1,), (0,)), ((), ())), preferred_element_type=F32)


def nt(a, b):
    return lax.dot_general(a, b, (((1,), (1,)), ((), ())), preferred_element_type=F32)


def tn(a, b):
    return lax.dot_general(a, b, (((0,), (0,)), ((), ())), preferred_element_type=F32)


def token_rows(x):
    return [8 * hi + 4 * b + x for b in range(2) for hi in range(4)]


def at(x):
    return slice(128 * x, 128 * (x + 1))


def norm(v):
    shifted = v - jnp.mean(v, axis=0, keepdims=True)
    inv = lax.rsqrt(jnp.mean(shifted * shifted, axis=0, keepdims=True) + EPSILON)
    return shifted * inv, inv


def norm_grad(dy, y, inv):
    return inv * (
        dy - jnp.mean(dy, axis=0, keepdims=True) - y * jnp.mean(dy * y, axis=0, keepdims=True)
    )


def halves(a, b):
    low = lax.broadcasted_iota(jnp.int32, a.shape, 1) < 64
    return jnp.where(low, a, pltpu.roll(b, 64, 1)), jnp.where(low, pltpu.roll(a, 64, 1), b)


def interchange(v):
    v = list(v)
    lane = lax.broadcasted_iota(jnp.int32, v[0].shape, 1)
    for bit in range(3):
        step = 16 << bit
        low = (lane & step) == 0
        for u in range(8):
            w = u | (1 << bit)
            if w == u:
                continue
            a, b = v[u], v[w]
            v[u] = jnp.where(low, a, pltpu.roll(b, step, 1))
            v[w] = jnp.where(low, pltpu.roll(a, 128 - step, 1), b)
    return v


def kernel(
    pair_ref, cot_ref, flags_ref, wio_ref, woo_ref, wii_ref, woi_ref,
    upd_ref, pg_ref, gio_ref, goo_ref, gii_ref, goi_ref,
    send, got, share, wide, mats, tall, mask_ref,
    z_ref, y_ref, yinv_ref, n_ref, proj_ref, gate_ref, t_ref, tinv_ref, tn_ref, lifted_ref,
    sides_ref, res_ref, lg_ref, pgr_ref, wint_ref, woutt_ref,
    ssem, rsem,
):
    cols = lax.axis_size("col")
    row, col = lax.axis_index("row"), lax.axis_index("col")
    me = row * cols + col

    def peer(step):
        other = lax.rem(me + step, N)
        return other // cols, lax.rem(other, cols)

    bar = pltpu.get_barrier_semaphore()

    @pl.loop(1, N)
    def _(step):
        pl.semaphore_signal(bar, inc=1, device_id=peer(step), device_id_type=MESH)

    def start(k):
        @pl.loop(1, N)
        def _(step):
            a, b = peer(step)
            pltpu.make_async_remote_copy(
                src_ref=send.at[k, a * cols + b], dst_ref=got.at[k, me], send_sem=ssem.at[k],
                recv_sem=rsem.at[k], device_id=(a, b), device_id_type=MESH,
            ).start()

        got[k, me] = send[k, me]

    def start_share(k, s):
        @pl.loop(1, N)
        def _(step):
            pltpu.make_async_remote_copy(
                src_ref=share.at[s], dst_ref=got.at[k, me], send_sem=ssem.at[k],
                recv_sem=rsem.at[k], device_id=peer(step), device_id_type=MESH,
            ).start()

        got[k, me] = share[s]

    def await_all(k, sem):
        part = got.at[k, pl.ds(0, N - 1)]
        pltpu.make_async_copy(part, part, sem.at[k]).wait()

    def put_pair(x, left, right):
        first, second = halves(left, right)
        wide[pl.ds(x, H, stride=8), :] = first
        wide[pl.ds(4 + x, H, stride=8), :] = second

    def pack(k):
        send[k] = wide[...].reshape(N, 8, 128).astype(BF16)

    def unpack(k):
        wide[...] = got[k].astype(F32).reshape(N * 8, 128)

    def take_pair(x):
        return halves(wide[pl.ds(x, H, stride=8), :], wide[pl.ds(4 + x, H, stride=8), :])

    def assemble(k):
        @pl.loop(0, 8)
        def _(r):
            for hi in range(2):
                v = interchange([got[k, r * 16 + hi * 8 + lo].astype(F32) for lo in range(8)])
                for t in range(2):
                    for ih in range(4):
                        rows = pl.ds(pl.multiple_of(r * 32 + ih * 8, 8), 8)
                        tall[t, rows, at(hi)] = v[t * 4 + ih]

    def disperse(k):
        @pl.loop(0, 8)
        def _(r):
            for hi in range(2):
                v = interchange([
                    tall[t, pl.ds(pl.multiple_of(r * 32 + ih * 8, 8), 8), at(hi)]
                    for t in range(2) for ih in range(4)
                ])
                for lo in range(8):
                    send[k, r * 16 + hi * 8 + lo] = v[lo].astype(BF16)

    def set_weights(w_in_ref, w_out_ref, s):
        wint_ref[s] = w_in_ref[...].astype(F32).T.astype(BF16)
        woutt_ref[s] = w_out_ref[...].astype(F32).T.astype(BF16)

    def project(s, k):
        for x in range(CHUNKS):
            y, inv = norm(z_ref[s, :, at(x)])
            y_ref[s, :, at(x)] = y
            yinv_ref[s, :, at(x)] = inv
            normed = y.astype(BF16)
            n_ref[s, :, at(x)] = normed
            mask = mask_ref[0:1, at(x)]
            p = nn(wint_ref[s], normed)
            proj_ref[s, :, at(x)] = p
            left = jax.nn.sigmoid(p[H : 2 * H]) * p[:H] * mask
            right = jax.nn.sigmoid(p[3 * H : 4 * H]) * p[2 * H : 3 * H] * mask
            put_pair(x, left, right)
        pack(k)
        start(k)
        gate_ref[s] = jax.nn.sigmoid(proj_ref[s, 4 * H :, :])

    def multiply(s, k_in, k_out, outgoing):
        await_all(k_in, rsem)
        assemble(k_in)
        mats[s] = tall[...].astype(BF16)
        if outgoing:
            tri = nt(mats[s, 0], mats[s, 1])
        else:
            tri = tn(mats[s, 0], mats[s, 1])
        high = tri.astype(BF16).astype(F32)
        tall[0] = high
        tall[1] = tri - high
        disperse(k_out)
        start(k_out)

    def lift(s, k, keep):
        await_all(k, rsem)
        unpack(k)
        for x in range(CHUNKS):
            high, low = take_pair(x)
            y, inv = norm(high + low)
            t_ref[s, :, at(x)] = y
            tinv_ref[s, :, at(x)] = inv
            normed = y.astype(BF16)
            tn_ref[s, :, at(x)] = normed
            lifted = nn(woutt_ref[s], normed)
            lifted_ref[s, :, at(x)] = lifted
            keep(x, (z_ref[s, :, at(x)] + gate_ref[s, :, at(x)] * lifted).astype(BF16))

    def back(s, w_out_ref, k):
        for x in range(CHUNKS):
            dres = res_ref[s, :, at(x)]
            lift_grad = (gate_ref[s, :, at(x)] * dres).astype(BF16)
            lg_ref[:, at(x)] = lift_grad
            dy = nn(w_out_ref[...], lift_grad)
            tri_grad = norm_grad(dy, t_ref[s, :, at(x)], tinv_ref[s, :, at(x)])
            put_pair(x, tri_grad, jnp.zeros_like(tri_grad))
        pack(k)
        start(k)

    def side_products(s, k_in, k_out, outgoing):
        await_all(k_in, rsem)
        assemble(k_in)
        grad = tall[0].astype(BF16)
        left, right = mats[s, 0], mats[s, 1]
        if outgoing:
            tall[0] = nn(grad, right)
            tall[1] = tn(grad, left)
        else:
            tall[0] = nt(right, grad)
            tall[1] = nn(left, grad)
        disperse(k_out)
        start(k_out)

    def unproject(s, w_in_ref, k, keep):
        await_all(k, rsem)
        unpack(k)
        for x in range(CHUNKS):
            left_grad, right_grad = take_pair(x)
            mask = mask_ref[0:1, at(x)]
            p = proj_ref[s, :, at(x)]
            dres = res_ref[s, :, at(x)]
            for side, grad in ((0, left_grad * mask), (2, right_grad * mask)):
                value = p[side * H : (side + 1) * H]
                sig = jax.nn.sigmoid(p[(side + 1) * H : (side + 2) * H])
                scaled = grad * sig
                pgr_ref[side * H : (side + 1) * H, at(x)] = scaled.astype(BF16)
                pgr_ref[(side + 1) * H : (side + 2) * H, at(x)] = (
                    scaled * value * (1.0 - sig)
                ).astype(BF16)
            gate = gate_ref[s, :, at(x)]
            pgr_ref[4 * H :, at(x)] = (
                lifted_ref[s, :, at(x)] * dres * gate * (1.0 - gate)
            ).astype(BF16)
            dy = nn(w_in_ref[...], pgr_ref[:, at(x)])
            grad = norm_grad(dy, y_ref[s, :, at(x)], yinv_ref[s, :, at(x)])
            keep(x, (dres + grad).astype(BF16))

    def sum_weights(s, k):
        w_in_grad = nt(n_ref[s], pgr_ref[...])
        for x in range(5):
            wide[pl.ds(x, H, stride=8), :] = w_in_grad[:, at(x)]
        wide[pl.ds(5, H, stride=8), :] = nt(tn_ref[s], lg_ref[...])
        wide[pl.ds(6, H, stride=8), :] = jnp.zeros((H, 128), F32)
        wide[pl.ds(7, H, stride=8), :] = jnp.zeros((H, 128), F32)
        pack(k)
        start(k)

    def share_weights(k_in, k_out, s):
        await_all(k_in, rsem)
        total = jnp.sum(got[k_in].astype(F32), axis=0)
        share[s] = (total * (1.0 / TOKENS)).astype(BF16)
        start_share(k_out, s)

    def give_weights(k, in_ref, out_ref):
        await_all(k, rsem)
        unpack(k)
        for x in range(5):
            in_ref[:, at(x)] = wide[pl.ds(x, H, stride=8), :]
        out_ref[...] = wide[pl.ds(5, H, stride=8), :]

    def write_tokens(ref, x, values):
        turned = values.astype(F32).T.astype(BF16)
        for m, i in enumerate(token_rows(x)):
            ref[i] = turned[16 * m : 16 * (m + 1)]

    def read_tokens(ref, x):
        return jnp.concatenate([ref[i] for i in token_rows(x)], axis=0).astype(F32).T

    lane = lax.broadcasted_iota(jnp.int32, (TOKENS, 512), 1)
    token = lax.broadcasted_iota(jnp.int32, (TOKENS, 512), 0)
    own_row = row * ROWS + ((lane >> 4) & 3) * 8 + ((lane >> 6) & 1) * 4 + (lane >> 7)
    own_col = col * COLS + (lane & 15)
    flags = jnp.broadcast_to(flags_ref[...].astype(F32), (8, TOKENS)).astype(BF16)
    row_flags = nn(flags, jnp.where(token == own_row, 1.0, 0.0).astype(BF16))
    col_flags = nn(flags, jnp.where(token == own_col, 1.0, 0.0).astype(BF16))
    mask_ref[...] = row_flags * col_flags

    set_weights(wio_ref, woo_ref, 0)
    for x in range(CHUNKS):
        z_ref[0, :, at(x)] = read_tokens(pair_ref, x)

    pl.semaphore_wait(bar, N - 1)
    project(0, OUT_LR)
    set_weights(wii_ref, woi_ref, 1)
    for x in range(CHUNKS):
        res_ref[1, :, at(x)] = read_tokens(cot_ref, x)
    multiply(0, OUT_LR, OUT_TRI, True)

    def keep_mid(x, mid):
        z_ref[1, :, at(x)] = mid.astype(F32)

    lift(0, OUT_TRI, keep_mid)
    project(1, IN_LR)
    multiply(1, IN_LR, IN_TRI, False)

    def keep_updated(x, updated):
        n_done = updated
        sides_ref[:, at(x)] = n_done

    lift(1, IN_TRI, keep_updated)
    back(1, woi_ref, IN_BACK)
    for x in range(CHUNKS):
        write_tokens(upd_ref, x, sides_ref[:, at(x)])
    side_products(1, IN_BACK, IN_SIDES, False)

    def keep_mid_grad(x, grad):
        res_ref[0, :, at(x)] = grad.astype(F32)

    unproject(1, wii_ref, IN_SIDES, keep_mid_grad)
    sum_weights(1, IN_SUM)
    back(0, woo_ref, OUT_BACK)
    side_products(0, OUT_BACK, OUT_SIDES, True)
    share_weights(IN_SUM, IN_SHARE, 0)

    def keep_pair_grad(x, grad):
        sides_ref[:, at(x)] = grad

    unproject(0, wio_ref, OUT_SIDES, keep_pair_grad)
    sum_weights(0, OUT_SUM)
    for x in range(CHUNKS):
        write_tokens(pg_ref, x, sides_ref[:, at(x)])
    give_weights(IN_SHARE, gii_ref, goi_ref)
    share_weights(OUT_SUM, OUT_SHARE, 1)
    give_weights(OUT_SHARE, gio_ref, goo_ref)
    for k in range(EXCHANGES):
        await_all(k, ssem)


def local(pair, cotangent, token_mask, out_in_proj, out_out_proj, in_in_proj, in_out_proj):
    tile = jax.ShapeDtypeStruct((ROWS, COLS, H), BF16)
    wide_grad = jax.ShapeDtypeStruct((H, 5 * H), F32)
    small_grad = jax.ShapeDtypeStruct((H, H), F32)
    vmem = pl.BlockSpec(memory_space=pltpu.VMEM)
    return pl.pallas_call(
        kernel,
        name="triangle_step",
        out_shape=(tile, tile, wide_grad, small_grad, wide_grad, small_grad),
        in_specs=[vmem] * 7,
        out_specs=(vmem,) * 6,
        scratch_shapes=[
            pltpu.VMEM((EXCHANGES, N, 8, 128), BF16),
            pltpu.VMEM((EXCHANGES, N, 8, 128), BF16),
            pltpu.VMEM((2, 8, 128), BF16),
            pltpu.VMEM((N * 8, 128), F32),
            pltpu.VMEM((2, 2, TOKENS, TOKENS), BF16),
            pltpu.VMEM((2, TOKENS, TOKENS), F32),
            pltpu.VMEM((8, 512), F32),
            pltpu.VMEM((2, H, 512), F32),
            pltpu.VMEM((2, H, 512), F32),
            pltpu.VMEM((2, 1, 512), F32),
            pltpu.VMEM((2, H, 512), BF16),
            pltpu.VMEM((2, 5 * H, 512), F32),
            pltpu.VMEM((2, H, 512), F32),
            pltpu.VMEM((2, H, 512), F32),
            pltpu.VMEM((2, 1, 512), F32),
            pltpu.VMEM((2, H, 512), BF16),
            pltpu.VMEM((2, H, 512), F32),
            pltpu.VMEM((H, 512), BF16),
            pltpu.VMEM((2, H, 512), F32),
            pltpu.VMEM((H, 512), BF16),
            pltpu.VMEM((5 * H, 512), BF16),
            pltpu.VMEM((2, 5 * H, H), BF16),
            pltpu.VMEM((2, H, H), BF16),
            pltpu.SemaphoreType.DMA((EXCHANGES,)),
            pltpu.SemaphoreType.DMA((EXCHANGES,)),
        ],
        compiler_params=pltpu.CompilerParams(
            collective_id=0, has_side_effects=True, vmem_limit_bytes=48 * 1024 * 1024
        ),
    )(
        pair, cotangent, token_mask.reshape(1, TOKENS),
        out_in_proj, out_out_proj, in_in_proj, in_out_proj,
    )


def solution(mesh):
    return jax.shard_map(
        local,
        mesh=mesh,
        in_specs=(P("row", "col", None), P("row", "col", None), P(), P(), P(), P(), P()),
        out_specs=(P("row", "col", None), P("row", "col", None), P(), P(), P(), P()),
        check_vma=False,
    )
```

```python
import jax
import jax.numpy as jnp
from jax import lax
from jax.experimental import pallas as pl
from jax.experimental.pallas import tpu as pltpu
from jax.sharding import PartitionSpec as P

MESH = pl.DeviceIdType.MESH
F32 = jnp.float32
BF16 = jnp.bfloat16
EPSILON = 1e-05
N = 128
H = 128
ROWS, COLS = 32, 16
CHUNKS = 4
TOKENS = 256
OUT_LR, OUT_TRI, IN_LR, IN_TRI, IN_BACK, IN_SIDES, OUT_BACK, OUT_SIDES = range(8)
IN_SUM, IN_SHARE, OUT_SUM, OUT_SHARE = range(8, 12)
EXCHANGES = 12


def nn(a, b):
    return lax.dot_general(a, b, (((1,), (0,)), ((), ())), preferred_element_type=F32)


def nt(a, b):
    return lax.dot_general(a, b, (((1,), (1,)), ((), ())), preferred_element_type=F32)


def tn(a, b):
    return lax.dot_general(a, b, (((0,), (0,)), ((), ())), preferred_element_type=F32)


def token_rows(x):
    return [8 * hi + 4 * b + x for b in range(2) for hi in range(4)]


def at(x):
    return slice(128 * x, 128 * (x + 1))


def norm(v):
    shifted = v - jnp.mean(v, axis=0, keepdims=True)
    inv = lax.rsqrt(jnp.mean(shifted * shifted, axis=0, keepdims=True) + EPSILON)
    return shifted * inv, inv


def norm_grad(dy, y, inv):
    return inv * (
        dy - jnp.mean(dy, axis=0, keepdims=True) - y * jnp.mean(dy * y, axis=0, keepdims=True)
    )


def halves(a, b):
    low = lax.broadcasted_iota(jnp.int32, a.shape, 1) < 64
    return jnp.where(low, a, pltpu.roll(b, 64, 1)), jnp.where(low, pltpu.roll(a, 64, 1), b)


def interchange(v):
    v = list(v)
    lane = lax.broadcasted_iota(jnp.int32, v[0].shape, 1)
    for bit in range(3):
        step = 16 << bit
        low = (lane & step) == 0
        for u in range(8):
            w = u | (1 << bit)
            if w == u:
                continue
            a, b = v[u], v[w]
            v[u] = jnp.where(low, a, pltpu.roll(b, step, 1))
            v[w] = jnp.where(low, pltpu.roll(a, 128 - step, 1), b)
    return v


def kernel(
    pair_in, cot_in, flags_in, wio_in, woo_in, wii_in, woi_in,
    upd_ref, pg_ref, gio_ref, goo_ref, gii_ref, goi_ref,
    send, got, share, wide, mats, tall, mask_ref,
    z_ref, y_ref, yinv_ref, n_ref, proj_ref, gate_ref, t_ref, tinv_ref, tn_ref, lifted_ref,
    sides_ref, res_ref, lg_ref, pgr_ref, wint_ref, woutt_ref,
    pair_ref, cot_ref, flags_ref, wio_ref, woo_ref, wii_ref, woi_ref,
    ssem, rsem, isem,
):
    loads = [
        pltpu.make_async_copy(src, dst, isem.at[n])
        for n, (src, dst) in enumerate((
            (pair_in, pair_ref), (wio_in, wio_ref), (flags_in, flags_ref), (woo_in, woo_ref),
            (cot_in, cot_ref), (wii_in, wii_ref), (woi_in, woi_ref),
        ))
    ]
    for load in loads:
        load.start()

    cols = lax.axis_size("col")
    row, col = lax.axis_index("row"), lax.axis_index("col")
    me = row * cols + col

    place_y, place_z, core = row // 2, col // 4, lax.rem(col, 2)
    place_x = lax.rem(col, 4) // 2 * 2 + lax.rem(row, 2)

    def peer(step):
        def turned(place, digit):
            return (place + (digit ^ (digit >> 1) ^ 2)) & 3

        z, x = turned(place_z, step >> 5), turned(place_x, (step >> 3) & 3)
        y, c = turned(place_y, (step >> 1) & 3), core ^ (step & 1) ^ 1
        return y * 2 + (x & 1), z * 4 + (x >> 1) * 2 + c

    bar = pltpu.get_barrier_semaphore()

    @pl.loop(0, N - 1)
    def _(step):
        pl.semaphore_signal(bar, inc=1, device_id=peer(step), device_id_type=MESH)

    def start(k):
        @pl.loop(0, N - 1)
        def _(step):
            a, b = peer(step)
            pltpu.make_async_remote_copy(
                src_ref=send.at[k, a * cols + b], dst_ref=got.at[k, me], send_sem=ssem.at[k],
                recv_sem=rsem.at[k], device_id=(a, b), device_id_type=MESH,
            ).start()

        got[k, me] = send[k, me]

    def start_share(k, s):
        @pl.loop(0, N - 1)
        def _(step):
            pltpu.make_async_remote_copy(
                src_ref=share.at[s], dst_ref=got.at[k, me], send_sem=ssem.at[k],
                recv_sem=rsem.at[k], device_id=peer(step), device_id_type=MESH,
            ).start()

        got[k, me] = share[s]

    def await_all(k, sem):
        part = got.at[k, pl.ds(0, N - 1)]
        pltpu.make_async_copy(part, part, sem.at[k]).wait()

    def put_pair(x, left, right):
        first, second = halves(left, right)
        wide[pl.ds(x, H, stride=8), :] = first
        wide[pl.ds(4 + x, H, stride=8), :] = second

    def pack(k):
        send[k] = wide[...].reshape(N, 8, 128).astype(BF16)

    def unpack(k):
        wide[...] = got[k].astype(F32).reshape(N * 8, 128)

    def take_pair(x):
        return halves(wide[pl.ds(x, H, stride=8), :], wide[pl.ds(4 + x, H, stride=8), :])

    def assemble(k):
        for r in range(8):
            for hi in range(2):
                v = interchange([got[k, r * 16 + hi * 8 + lo].astype(F32) for lo in range(8)])
                for t in range(2):
                    for ih in range(4):
                        rows = slice(r * 32 + ih * 8, r * 32 + ih * 8 + 8)
                        tall[t, rows, at(hi)] = v[t * 4 + ih]

    def disperse(k):
        for r in range(8):
            for hi in range(2):
                v = interchange([
                    tall[t, slice(r * 32 + ih * 8, r * 32 + ih * 8 + 8), at(hi)]
                    for t in range(2) for ih in range(4)
                ])
                for lo in range(8):
                    send[k, r * 16 + hi * 8 + lo] = v[lo].astype(BF16)

    def set_in(w_in_ref, s):
        wint_ref[s] = w_in_ref[...].astype(F32).T.astype(BF16)

    def set_out(w_out_ref, s):
        woutt_ref[s] = w_out_ref[...].astype(F32).T.astype(BF16)

    def project(s, k, ready=lambda: None):
        for x in range(CHUNKS):
            y, inv = norm(z_ref[s, :, at(x)])
            y_ref[s, :, at(x)] = y
            yinv_ref[s, :, at(x)] = inv
            normed = y.astype(BF16)
            n_ref[s, :, at(x)] = normed
            mask = mask_ref[0:1, at(x)]
            p = nn(wint_ref[s], normed)
            proj_ref[s, :, at(x)] = p
            left = jax.nn.sigmoid(p[H : 2 * H]) * p[:H] * mask
            right = jax.nn.sigmoid(p[3 * H : 4 * H]) * p[2 * H : 3 * H] * mask
            put_pair(x, left, right)
        pack(k)
        ready()
        start(k)
        gate_ref[s] = jax.nn.sigmoid(proj_ref[s, 4 * H :, :])

    def multiply(s, k_in, k_out, outgoing):
        await_all(k_in, rsem)
        assemble(k_in)
        mats[s] = tall[...].astype(BF16)
        if outgoing:
            tri = nt(mats[s, 0], mats[s, 1])
        else:
            tri = tn(mats[s, 0], mats[s, 1])
        high = tri.astype(BF16).astype(F32)
        tall[0] = high
        tall[1] = tri - high
        disperse(k_out)
        start(k_out)

    def lift(s, k, keep):
        await_all(k, rsem)
        unpack(k)
        for x in range(CHUNKS):
            high, low = take_pair(x)
            y, inv = norm(high + low)
            t_ref[s, :, at(x)] = y
            tinv_ref[s, :, at(x)] = inv
            normed = y.astype(BF16)
            tn_ref[s, :, at(x)] = normed
            lifted = nn(woutt_ref[s], normed)
            lifted_ref[s, :, at(x)] = lifted
            keep(x, (z_ref[s, :, at(x)] + gate_ref[s, :, at(x)] * lifted).astype(BF16))

    def back(s, w_out_ref, k):
        for x in range(CHUNKS):
            dres = res_ref[s, :, at(x)]
            lift_grad = (gate_ref[s, :, at(x)] * dres).astype(BF16)
            lg_ref[s, :, at(x)] = lift_grad
            dy = nn(w_out_ref[...], lift_grad)
            tri_grad = norm_grad(dy, t_ref[s, :, at(x)], tinv_ref[s, :, at(x)])
            put_pair(x, tri_grad, jnp.zeros_like(tri_grad))
        pack(k)
        start(k)

    def side_products(s, k_in, k_out, outgoing):
        await_all(k_in, rsem)
        assemble(k_in)
        grad = tall[0].astype(BF16)
        left, right = mats[s, 0], mats[s, 1]
        if outgoing:
            tall[0] = nn(grad, right)
            tall[1] = tn(grad, left)
        else:
            tall[0] = nt(right, grad)
            tall[1] = nn(left, grad)
        disperse(k_out)
        start(k_out)

    def unproject(s, w_in_ref, k, keep):
        await_all(k, rsem)
        unpack(k)
        for x in range(CHUNKS):
            left_grad, right_grad = take_pair(x)
            mask = mask_ref[0:1, at(x)]
            p = proj_ref[s, :, at(x)]
            dres = res_ref[s, :, at(x)]
            for side, grad in ((0, left_grad * mask), (2, right_grad * mask)):
                value = p[side * H : (side + 1) * H]
                sig = jax.nn.sigmoid(p[(side + 1) * H : (side + 2) * H])
                scaled = grad * sig
                pgr_ref[side * H : (side + 1) * H, at(x)] = scaled.astype(BF16)
                pgr_ref[(side + 1) * H : (side + 2) * H, at(x)] = (
                    scaled * value * (1.0 - sig)
                ).astype(BF16)
            gate = gate_ref[s, :, at(x)]
            pgr_ref[4 * H :, at(x)] = (
                lifted_ref[s, :, at(x)] * dres * gate * (1.0 - gate)
            ).astype(BF16)
            dy = nn(w_in_ref[...], pgr_ref[:, at(x)])
            grad = norm_grad(dy, y_ref[s, :, at(x)], yinv_ref[s, :, at(x)])
            keep(x, (dres + grad).astype(BF16))

    def sum_weights(s, k):
        w_in_grad = nt(n_ref[s], pgr_ref[...])
        for x in range(5):
            wide[pl.ds(x, H, stride=8), :] = w_in_grad[:, at(x)]
        wide[pl.ds(5, H, stride=8), :] = nt(tn_ref[s], lg_ref[s])
        wide[pl.ds(6, H, stride=8), :] = jnp.zeros((H, 128), F32)
        wide[pl.ds(7, H, stride=8), :] = jnp.zeros((H, 128), F32)
        pack(k)
        start(k)

    def share_weights(k_in, k_out, s):
        await_all(k_in, rsem)
        total = jnp.sum(got[k_in].astype(F32), axis=0)
        share[s] = (total * (1.0 / TOKENS)).astype(BF16)
        start_share(k_out, s)

    def give_weights(k, in_ref, out_ref):
        await_all(k, rsem)
        unpack(k)
        for x in range(5):
            in_ref[:, at(x)] = wide[pl.ds(x, H, stride=8), :]
        out_ref[...] = wide[pl.ds(5, H, stride=8), :]

    def write_tokens(ref, x, values):
        turned = values.astype(F32).T.astype(BF16)
        for m, i in enumerate(token_rows(x)):
            ref[i] = turned[16 * m : 16 * (m + 1)]

    def read_tokens(ref, x):
        return jnp.concatenate([ref[i] for i in token_rows(x)], axis=0).astype(F32).T

    for load in loads[:3]:
        load.wait()

    lane = lax.broadcasted_iota(jnp.int32, (TOKENS, 512), 1)
    token = lax.broadcasted_iota(jnp.int32, (TOKENS, 512), 0)
    own_row = row * ROWS + ((lane >> 4) & 3) * 8 + ((lane >> 6) & 1) * 4 + (lane >> 7)
    own_col = col * COLS + (lane & 15)
    flags = jnp.broadcast_to(flags_ref[...].astype(F32), (8, TOKENS)).astype(BF16)
    row_flags = nn(flags, jnp.where(token == own_row, 1.0, 0.0).astype(BF16))
    col_flags = nn(flags, jnp.where(token == own_col, 1.0, 0.0).astype(BF16))
    mask_ref[...] = row_flags * col_flags

    set_in(wio_ref, 0)
    for x in range(CHUNKS):
        z_ref[0, :, at(x)] = read_tokens(pair_ref, x)

    project(0, OUT_LR, lambda: pl.semaphore_wait(bar, N - 1))
    for load in loads[3:]:
        load.wait()
    set_out(woo_ref, 0)
    set_in(wii_ref, 1)
    set_out(woi_ref, 1)
    for x in range(CHUNKS):
        res_ref[1, :, at(x)] = read_tokens(cot_ref, x)
    multiply(0, OUT_LR, OUT_TRI, True)

    def keep_mid(x, mid):
        z_ref[1, :, at(x)] = mid.astype(F32)

    lift(0, OUT_TRI, keep_mid)
    project(1, IN_LR)
    multiply(1, IN_LR, IN_TRI, False)

    def keep_updated(x, updated):
        sides_ref[:, at(x)] = updated

    lift(1, IN_TRI, keep_updated)
    back(1, woi_ref, IN_BACK)
    for x in range(CHUNKS):
        write_tokens(upd_ref, x, sides_ref[:, at(x)])
    side_products(1, IN_BACK, IN_SIDES, False)

    def keep_mid_grad(x, grad):
        res_ref[0, :, at(x)] = grad.astype(F32)

    unproject(1, wii_ref, IN_SIDES, keep_mid_grad)
    back(0, woo_ref, OUT_BACK)
    sum_weights(1, IN_SUM)
    side_products(0, OUT_BACK, OUT_SIDES, True)
    share_weights(IN_SUM, IN_SHARE, 0)

    def keep_pair_grad(x, grad):
        sides_ref[:, at(x)] = grad

    unproject(0, wio_ref, OUT_SIDES, keep_pair_grad)
    sum_weights(0, OUT_SUM)
    for x in range(CHUNKS):
        write_tokens(pg_ref, x, sides_ref[:, at(x)])
    give_weights(IN_SHARE, gii_ref, goi_ref)
    share_weights(OUT_SUM, OUT_SHARE, 1)
    give_weights(OUT_SHARE, gio_ref, goo_ref)
    for k in range(EXCHANGES):
        await_all(k, ssem)


def deliver(*refs):
    copies = [
        pltpu.make_async_copy(refs[n], refs[6 + n], refs[12].at[n]) for n in (2, 4, 0, 1, 3, 5)
    ]
    for copy in copies:
        copy.start()
    for copy in copies:
        copy.wait()


def local(pair, cotangent, token_mask, out_in_proj, out_out_proj, in_in_proj, in_out_proj):
    tile = jax.ShapeDtypeStruct((ROWS, COLS, H), BF16)
    wide_grad = jax.ShapeDtypeStruct((H, 5 * H), F32)
    small_grad = jax.ShapeDtypeStruct((H, H), F32)
    vmem = pl.BlockSpec(memory_space=pltpu.VMEM)
    far = pl.BlockSpec(memory_space=pltpu.HBM)
    shapes = (tile, tile, wide_grad, small_grad, wide_grad, small_grad)
    results = pl.pallas_call(
        kernel,
        name="triangle_step",
        out_shape=tuple(pltpu.VMEM(s.shape, s.dtype) for s in shapes),
        in_specs=[far] * 7,
        out_specs=(vmem,) * 6,
        scratch_shapes=[
            pltpu.VMEM((EXCHANGES, N, 8, 128), BF16),
            pltpu.VMEM((EXCHANGES, N, 8, 128), BF16),
            pltpu.VMEM((2, 8, 128), BF16),
            pltpu.VMEM((N * 8, 128), F32),
            pltpu.VMEM((2, 2, TOKENS, TOKENS), BF16),
            pltpu.VMEM((2, TOKENS, TOKENS), F32),
            pltpu.VMEM((8, 512), F32),
            pltpu.VMEM((2, H, 512), F32),
            pltpu.VMEM((2, H, 512), F32),
            pltpu.VMEM((2, 1, 512), F32),
            pltpu.VMEM((2, H, 512), BF16),
            pltpu.VMEM((2, 5 * H, 512), F32),
            pltpu.VMEM((2, H, 512), F32),
            pltpu.VMEM((2, H, 512), F32),
            pltpu.VMEM((2, 1, 512), F32),
            pltpu.VMEM((2, H, 512), BF16),
            pltpu.VMEM((2, H, 512), F32),
            pltpu.VMEM((H, 512), BF16),
            pltpu.VMEM((2, H, 512), F32),
            pltpu.VMEM((2, H, 512), BF16),
            pltpu.VMEM((5 * H, 512), BF16),
            pltpu.VMEM((2, 5 * H, H), BF16),
            pltpu.VMEM((2, H, H), BF16),
            pltpu.VMEM((ROWS, COLS, H), BF16),
            pltpu.VMEM((ROWS, COLS, H), BF16),
            pltpu.VMEM((1, TOKENS), jnp.int32),
            pltpu.VMEM((H, 5 * H), BF16),
            pltpu.VMEM((H, H), BF16),
            pltpu.VMEM((H, 5 * H), BF16),
            pltpu.VMEM((H, H), BF16),
            pltpu.SemaphoreType.DMA((EXCHANGES,)),
            pltpu.SemaphoreType.DMA((EXCHANGES,)),
            pltpu.SemaphoreType.DMA((7,)),
        ],
        compiler_params=pltpu.CompilerParams(
            collective_id=0, has_side_effects=True, vmem_limit_bytes=40 * 1024 * 1024
        ),
    )(*(
        pltpu.with_memory_space_constraint(array, pltpu.HBM)
        for array in (
            pair, cotangent, token_mask.reshape(1, TOKENS),
            out_in_proj, out_out_proj, in_in_proj, in_out_proj,
        )
    ))
    results = [pltpu.with_memory_space_constraint(r, pltpu.VMEM) for r in results]
    return pl.pallas_call(
        deliver,
        name="deliver",
        out_shape=shapes,
        in_specs=[vmem] * 6,
        out_specs=(far,) * 6,
        scratch_shapes=[pltpu.SemaphoreType.DMA((6,))],
    )(*results)


def solution(mesh):
    return jax.shard_map(
        local,
        mesh=mesh,
        in_specs=(P("row", "col", None), P("row", "col", None), P(), P(), P(), P(), P()),
        out_specs=(P("row", "col", None), P("row", "col", None), P(), P(), P(), P()),
        check_vma=False,
    )
```

```python
import jax
import jax.numpy as jnp
from jax import lax
from jax.experimental import pallas as pl
from jax.experimental.pallas import tpu as pltpu
from jax.sharding import PartitionSpec as P

MESH = pl.DeviceIdType.MESH
F32 = jnp.float32
BF16 = jnp.bfloat16
EPSILON = 1e-05
N = 128
H = 128
ROWS, COLS = 32, 16
CHUNKS = 4
TOKENS = 256
OUT_LR, IN_LR, IN_SIDES, OUT_SIDES, IN_SUM, IN_SHARE = range(6)
OUT_TRI, IN_TRI, IN_BACK, OUT_BACK, OUT_SUM, OUT_SHARE = range(6, 12)
EXCHANGES = 12


def nn(a, b):
    return lax.dot_general(a, b, (((1,), (0,)), ((), ())), preferred_element_type=F32)


def nt(a, b):
    return lax.dot_general(a, b, (((1,), (1,)), ((), ())), preferred_element_type=F32)


def tn(a, b):
    return lax.dot_general(a, b, (((0,), (0,)), ((), ())), preferred_element_type=F32)


def token_rows(x):
    return [8 * hi + 4 * b + x for b in range(2) for hi in range(4)]


def at(x):
    return slice(128 * x, 128 * (x + 1))


def norm(v):
    shifted = v - jnp.mean(v, axis=0, keepdims=True)
    inv = lax.rsqrt(jnp.mean(shifted * shifted, axis=0, keepdims=True) + EPSILON)
    return shifted * inv, inv


def norm_grad(dy, y, inv):
    return inv * (
        dy - jnp.mean(dy, axis=0, keepdims=True) - y * jnp.mean(dy * y, axis=0, keepdims=True)
    )


def halves(a, b):
    low = lax.broadcasted_iota(jnp.int32, a.shape, 1) < 64
    return jnp.where(low, a, pltpu.roll(b, 64, 1)), jnp.where(low, pltpu.roll(a, 64, 1), b)


def interchange(v):
    v = list(v)
    lane = lax.broadcasted_iota(jnp.int32, v[0].shape, 1)
    for bit in range(3):
        step = 16 << bit
        low = (lane & step) == 0
        for u in range(8):
            w = u | (1 << bit)
            if w == u:
                continue
            a, b = v[u], v[w]
            v[u] = jnp.where(low, a, pltpu.roll(b, step, 1))
            v[w] = jnp.where(low, pltpu.roll(a, 128 - step, 1), b)
    return v


def kernel(
    pair_in, cot_in, flags_in, wio_in, woo_in, wii_in, woi_in,
    upd_ref, pg_ref, gio_ref, goo_ref, gii_ref, goi_ref,
    send8, got8, send4, got4, share8, share4, wide, mats, tall, mask_ref,
    z_ref, y_ref, yinv_ref, n_ref, proj_ref, gate_ref, t_ref, tinv_ref, tn_ref, lifted_ref,
    sides_ref, res_ref, lg_ref, pgr_ref, wint_ref, woutt_ref,
    pair_ref, cot_ref, flags_ref, wio_ref, woo_ref, wii_ref, woi_ref,
    ssem, rsem, isem,
):
    loads = [
        pltpu.make_async_copy(src, dst, isem.at[n])
        for n, (src, dst) in enumerate((
            (pair_in, pair_ref), (wio_in, wio_ref), (flags_in, flags_ref), (woo_in, woo_ref),
            (cot_in, cot_ref), (wii_in, wii_ref), (woi_in, woi_ref),
        ))
    ]
    for load in loads:
        load.start()

    cols = lax.axis_size("col")
    row, col = lax.axis_index("row"), lax.axis_index("col")
    me = row * cols + col

    place_y, place_z, core = row // 2, col // 4, lax.rem(col, 2)
    place_x = lax.rem(col, 4) // 2 * 2 + lax.rem(row, 2)

    def peer(step):
        def turned(place, digit):
            return (place + (digit ^ (digit >> 1) ^ 2)) & 3

        z, x = turned(place_z, step >> 5), turned(place_x, (step >> 3) & 3)
        y, c = turned(place_y, (step >> 1) & 3), core ^ (step & 1) ^ 1
        return y * 2 + (x & 1), z * 4 + (x >> 1) * 2 + c

    bar = pltpu.get_barrier_semaphore()

    @pl.loop(0, N - 1)
    def _(step):
        pl.semaphore_signal(bar, inc=1, device_id=peer(step), device_id_type=MESH)

    def sent(k):
        return send8.at[k] if k < 6 else send4.at[k - 6]

    def got(k):
        return got8.at[k] if k < 6 else got4.at[k - 6]

    def start(k):
        source, target = sent(k), got(k)

        @pl.loop(0, N - 1)
        def _(step):
            a, b = peer(step)
            pltpu.make_async_remote_copy(
                src_ref=source.at[a * cols + b], dst_ref=target.at[me], send_sem=ssem.at[k],
                recv_sem=rsem.at[k], device_id=(a, b), device_id_type=MESH,
            ).start()

        target[me] = source[me]

    def start_share(k):
        source, target = share8 if k < 6 else share4, got(k)

        @pl.loop(0, N - 1)
        def _(step):
            pltpu.make_async_remote_copy(
                src_ref=source, dst_ref=target.at[me], send_sem=ssem.at[k],
                recv_sem=rsem.at[k], device_id=peer(step), device_id_type=MESH,
            ).start()

        target[me] = source[...]

    def await_all(k, sem):
        part = got(k).at[pl.ds(0, N - 1)]
        pltpu.make_async_copy(part, part, sem.at[k]).wait()

    def put_pair(x, left, right):
        first, second = halves(left, right)
        wide[pl.ds(x, H, stride=8), :] = first
        wide[pl.ds(4 + x, H, stride=8), :] = second

    def put(x, value):
        wide[pl.ds(x, H, stride=4), :] = value

    def pack(k):
        if k < 6:
            sent(k)[...] = wide[...].reshape(N, 8, 128).astype(BF16)
            return
        for pair in range(N // 2):
            both = wide[8 * pair : 8 * pair + 8, :]
            sent(k)[2 * pair] = both[:4].astype(BF16)
            sent(k)[2 * pair + 1] = both[4:].astype(BF16)

    def unpack(k):
        if k < 6:
            wide[...] = got(k)[...].astype(F32).reshape(N * 8, 128)
            return
        for n in range(N):
            wide[4 * n : 4 * n + 4, :] = got(k)[n].astype(F32)

    def take_pair(x):
        return halves(wide[pl.ds(x, H, stride=8), :], wide[pl.ds(4 + x, H, stride=8), :])

    def take(x):
        return wide[pl.ds(x, H, stride=4), :]

    def spots(k, r, hi):
        if k < 6:
            return [
                (t, slice(r * 32 + ih * 8, r * 32 + ih * 8 + 8), at(hi))
                for t in range(2) for ih in range(4)
            ]
        return [
            (0, slice(r * 32 + ih * 8 + b * 4, r * 32 + ih * 8 + b * 4 + 4), at(hi))
            for b in range(2) for ih in range(4)
        ]

    def assemble(k):
        for r in range(8):
            for hi in range(2):
                v = interchange([got(k)[r * 16 + hi * 8 + lo].astype(F32) for lo in range(8)])
                for spot, part in zip(spots(k, r, hi), v):
                    tall[spot] = part

    def disperse(k):
        for r in range(8):
            for hi in range(2):
                v = interchange([tall[spot] for spot in spots(k, r, hi)])
                for lo in range(8):
                    sent(k)[r * 16 + hi * 8 + lo] = v[lo].astype(BF16)

    def set_in(w_in_ref, s):
        wint_ref[s] = w_in_ref[...].astype(F32).T.astype(BF16)

    def set_out(w_out_ref, s):
        woutt_ref[s] = w_out_ref[...].astype(F32).T.astype(BF16)

    def project(s, k, ready=lambda: None):
        for x in range(CHUNKS):
            y, inv = norm(z_ref[s, :, at(x)])
            y_ref[s, :, at(x)] = y
            yinv_ref[s, :, at(x)] = inv
            normed = y.astype(BF16)
            n_ref[s, :, at(x)] = normed
            mask = mask_ref[0:1, at(x)]
            p = nn(wint_ref[s], normed)
            proj_ref[s, :, at(x)] = p
            left = jax.nn.sigmoid(p[H : 2 * H]) * p[:H] * mask
            right = jax.nn.sigmoid(p[3 * H : 4 * H]) * p[2 * H : 3 * H] * mask
            put_pair(x, left, right)
        pack(k)
        ready()
        start(k)
        gate_ref[s] = jax.nn.sigmoid(proj_ref[s, 4 * H :, :])

    def multiply(s, k_in, k_out, outgoing):
        await_all(k_in, rsem)
        assemble(k_in)
        mats[s] = tall[...].astype(BF16)
        if outgoing:
            tall[0] = nt(mats[s, 0], mats[s, 1])
        else:
            tall[0] = tn(mats[s, 0], mats[s, 1])
        disperse(k_out)
        start(k_out)

    def lift(s, k, keep):
        await_all(k, rsem)
        unpack(k)
        for x in range(CHUNKS):
            y, inv = norm(take(x))
            t_ref[s, :, at(x)] = y
            tinv_ref[s, :, at(x)] = inv
            normed = y.astype(BF16)
            tn_ref[s, :, at(x)] = normed
            lifted = nn(woutt_ref[s], normed)
            lifted_ref[s, :, at(x)] = lifted
            keep(x, (z_ref[s, :, at(x)] + gate_ref[s, :, at(x)] * lifted).astype(BF16))

    def back(s, w_out_ref, k):
        for x in range(CHUNKS):
            dres = res_ref[s, :, at(x)]
            lift_grad = (gate_ref[s, :, at(x)] * dres).astype(BF16)
            lg_ref[s, :, at(x)] = lift_grad
            dy = nn(w_out_ref[...], lift_grad)
            tri_grad = norm_grad(dy, t_ref[s, :, at(x)], tinv_ref[s, :, at(x)])
            put(x, tri_grad)
        pack(k)
        start(k)
        for x in range(CHUNKS):
            gate = gate_ref[s, :, at(x)]
            pgr_ref[s, 4 * H :, at(x)] = (
                lifted_ref[s, :, at(x)] * res_ref[s, :, at(x)] * gate * (1.0 - gate)
            ).astype(BF16)

    def side_products(s, k_in, k_out, outgoing):
        await_all(k_in, rsem)
        assemble(k_in)
        grad = tall[0].astype(BF16)
        left, right = mats[s, 0], mats[s, 1]
        if outgoing:
            tall[0] = nn(grad, right)
            tall[1] = tn(grad, left)
        else:
            tall[0] = nt(right, grad)
            tall[1] = nn(left, grad)
        disperse(k_out)
        start(k_out)

    def unproject(s, w_in_ref, k, keep):
        await_all(k, rsem)
        unpack(k)
        for x in range(CHUNKS):
            left_grad, right_grad = take_pair(x)
            mask = mask_ref[0:1, at(x)]
            p = proj_ref[s, :, at(x)]
            dres = res_ref[s, :, at(x)]
            for side, grad in ((0, left_grad * mask), (2, right_grad * mask)):
                value = p[side * H : (side + 1) * H]
                sig = jax.nn.sigmoid(p[(side + 1) * H : (side + 2) * H])
                scaled = grad * sig
                pgr_ref[s, side * H : (side + 1) * H, at(x)] = scaled.astype(BF16)
                pgr_ref[s, (side + 1) * H : (side + 2) * H, at(x)] = (
                    scaled * value * (1.0 - sig)
                ).astype(BF16)
            dy = nn(w_in_ref[...], pgr_ref[s, :, at(x)])
            grad = norm_grad(dy, y_ref[s, :, at(x)], yinv_ref[s, :, at(x)])
            keep(x, (dres + grad).astype(BF16))

    def sum_early():
        w_in_grad = nt(n_ref[1], pgr_ref[1])
        for x in range(5):
            wide[pl.ds(x, H, stride=8), :] = w_in_grad[:, at(x)]
        wide[pl.ds(5, H, stride=8), :] = nt(tn_ref[1], lg_ref[1])
        wide[pl.ds(6, H, stride=8), :] = nt(tn_ref[0], lg_ref[0])
        wide[pl.ds(7, H, stride=8), :] = nt(n_ref[0], pgr_ref[0, 4 * H :, :])
        pack(IN_SUM)
        start(IN_SUM)

    def sum_late():
        w_in_grad = nt(n_ref[0], pgr_ref[0, : 4 * H, :])
        for x in range(4):
            put(x, w_in_grad[:, at(x)])
        pack(OUT_SUM)
        start(OUT_SUM)

    def share_sums(k_in, k_out):
        await_all(k_in, rsem)
        total = jnp.sum(got(k_in)[...].astype(F32), axis=0) * (1.0 / TOKENS)
        if k_in < 6:
            share8[...] = total.astype(BF16)
        else:
            share4[...] = total.astype(BF16)
        start_share(k_out)

    def give_early():
        await_all(IN_SHARE, rsem)
        unpack(IN_SHARE)
        for x in range(5):
            gii_ref[:, at(x)] = wide[pl.ds(x, H, stride=8), :]
        goi_ref[...] = wide[pl.ds(5, H, stride=8), :]
        goo_ref[...] = wide[pl.ds(6, H, stride=8), :]
        gio_ref[:, at(4)] = wide[pl.ds(7, H, stride=8), :]

    def give_late():
        await_all(OUT_SHARE, rsem)
        unpack(OUT_SHARE)
        for x in range(4):
            gio_ref[:, at(x)] = take(x)

    def write_tokens(ref, x, values):
        turned = values.astype(F32).T.astype(BF16)
        for m, i in enumerate(token_rows(x)):
            ref[i] = turned[16 * m : 16 * (m + 1)]

    def read_tokens(ref, x):
        return jnp.concatenate([ref[i] for i in token_rows(x)], axis=0).astype(F32).T

    for load in loads[:3]:
        load.wait()

    lane = lax.broadcasted_iota(jnp.int32, (TOKENS, 512), 1)
    token = lax.broadcasted_iota(jnp.int32, (TOKENS, 512), 0)
    own_row = row * ROWS + ((lane >> 4) & 3) * 8 + ((lane >> 6) & 1) * 4 + (lane >> 7)
    own_col = col * COLS + (lane & 15)
    flags = jnp.broadcast_to(flags_ref[...].astype(F32), (8, TOKENS)).astype(BF16)
    row_flags = nn(flags, jnp.where(token == own_row, 1.0, 0.0).astype(BF16))
    col_flags = nn(flags, jnp.where(token == own_col, 1.0, 0.0).astype(BF16))
    mask_ref[...] = row_flags * col_flags

    set_in(wio_ref, 0)
    for x in range(CHUNKS):
        z_ref[0, :, at(x)] = read_tokens(pair_ref, x)

    project(0, OUT_LR, lambda: pl.semaphore_wait(bar, N - 1))
    for load in loads[3:]:
        load.wait()
    set_out(woo_ref, 0)
    set_in(wii_ref, 1)
    set_out(woi_ref, 1)
    for x in range(CHUNKS):
        res_ref[1, :, at(x)] = read_tokens(cot_ref, x)
    multiply(0, OUT_LR, OUT_TRI, True)

    def keep_mid(x, mid):
        z_ref[1, :, at(x)] = mid.astype(F32)

    lift(0, OUT_TRI, keep_mid)
    project(1, IN_LR)
    multiply(1, IN_LR, IN_TRI, False)

    def keep_updated(x, updated):
        sides_ref[:, at(x)] = updated

    lift(1, IN_TRI, keep_updated)
    back(1, woi_ref, IN_BACK)
    for x in range(CHUNKS):
        write_tokens(upd_ref, x, sides_ref[:, at(x)])
    side_products(1, IN_BACK, IN_SIDES, False)

    def keep_mid_grad(x, grad):
        res_ref[0, :, at(x)] = grad.astype(F32)

    unproject(1, wii_ref, IN_SIDES, keep_mid_grad)
    back(0, woo_ref, OUT_BACK)
    sum_early()
    side_products(0, OUT_BACK, OUT_SIDES, True)
    share_sums(IN_SUM, IN_SHARE)

    def keep_pair_grad(x, grad):
        sides_ref[:, at(x)] = grad

    unproject(0, wio_ref, OUT_SIDES, keep_pair_grad)
    sum_late()
    for x in range(CHUNKS):
        write_tokens(pg_ref, x, sides_ref[:, at(x)])
    give_early()
    share_sums(OUT_SUM, OUT_SHARE)
    give_late()
    for k in range(EXCHANGES):
        await_all(k, ssem)


def deliver(*refs):
    copies = [
        pltpu.make_async_copy(refs[n], refs[6 + n], refs[12].at[n]) for n in (2, 4, 0, 1, 3, 5)
    ]
    for copy in copies:
        copy.start()
    for copy in copies:
        copy.wait()


def local(pair, cotangent, token_mask, out_in_proj, out_out_proj, in_in_proj, in_out_proj):
    tile = jax.ShapeDtypeStruct((ROWS, COLS, H), BF16)
    wide_grad = jax.ShapeDtypeStruct((H, 5 * H), F32)
    small_grad = jax.ShapeDtypeStruct((H, H), F32)
    vmem = pl.BlockSpec(memory_space=pltpu.VMEM)
    far = pl.BlockSpec(memory_space=pltpu.HBM)
    shapes = (tile, tile, wide_grad, small_grad, wide_grad, small_grad)
    results = pl.pallas_call(
        kernel,
        name="triangle_step",
        out_shape=tuple(pltpu.VMEM(s.shape, s.dtype) for s in shapes),
        in_specs=[far] * 7,
        out_specs=(vmem,) * 6,
        scratch_shapes=[
            pltpu.VMEM((6, N, 8, 128), BF16),
            pltpu.VMEM((6, N, 8, 128), BF16),
            pltpu.VMEM((6, N, 4, 128), BF16),
            pltpu.VMEM((6, N, 4, 128), BF16),
            pltpu.VMEM((8, 128), BF16),
            pltpu.VMEM((4, 128), BF16),
            pltpu.VMEM((N * 8, 128), F32),
            pltpu.VMEM((2, 2, TOKENS, TOKENS), BF16),
            pltpu.VMEM((2, TOKENS, TOKENS), F32),
            pltpu.VMEM((8, 512), F32),
            pltpu.VMEM((2, H, 512), F32),
            pltpu.VMEM((2, H, 512), F32),
            pltpu.VMEM((2, 1, 512), F32),
            pltpu.VMEM((2, H, 512), BF16),
            pltpu.VMEM((2, 5 * H, 512), F32),
            pltpu.VMEM((2, H, 512), F32),
            pltpu.VMEM((2, H, 512), F32),
            pltpu.VMEM((2, 1, 512), F32),
            pltpu.VMEM((2, H, 512), BF16),
            pltpu.VMEM((2, H, 512), F32),
            pltpu.VMEM((H, 512), BF16),
            pltpu.VMEM((2, H, 512), F32),
            pltpu.VMEM((2, H, 512), BF16),
            pltpu.VMEM((2, 5 * H, 512), BF16),
            pltpu.VMEM((2, 5 * H, H), BF16),
            pltpu.VMEM((2, H, H), BF16),
            pltpu.VMEM((ROWS, COLS, H), BF16),
            pltpu.VMEM((ROWS, COLS, H), BF16),
            pltpu.VMEM((1, TOKENS), jnp.int32),
            pltpu.VMEM((H, 5 * H), BF16),
            pltpu.VMEM((H, H), BF16),
            pltpu.VMEM((H, 5 * H), BF16),
            pltpu.VMEM((H, H), BF16),
            pltpu.SemaphoreType.DMA((EXCHANGES,)),
            pltpu.SemaphoreType.DMA((EXCHANGES,)),
            pltpu.SemaphoreType.DMA((7,)),
        ],
        compiler_params=pltpu.CompilerParams(
            collective_id=0, has_side_effects=True, vmem_limit_bytes=40 * 1024 * 1024
        ),
    )(*(
        pltpu.with_memory_space_constraint(array, pltpu.HBM)
        for array in (
            pair, cotangent, token_mask.reshape(1, TOKENS),
            out_in_proj, out_out_proj, in_in_proj, in_out_proj,
        )
    ))
    results = [pltpu.with_memory_space_constraint(r, pltpu.VMEM) for r in results]
    return pl.pallas_call(
        deliver,
        name="deliver",
        out_shape=shapes,
        in_specs=[vmem] * 6,
        out_specs=(far,) * 6,
        scratch_shapes=[pltpu.SemaphoreType.DMA((6,))],
    )(*results)


def solution(mesh):
    return jax.shard_map(
        local,
        mesh=mesh,
        in_specs=(P("row", "col", None), P("row", "col", None), P(), P(), P(), P(), P()),
        out_specs=(P("row", "col", None), P("row", "col", None), P(), P(), P(), P()),
        check_vma=False,
    )
```

```python
import jax
import jax.numpy as jnp
from jax import lax
from jax.experimental import pallas as pl
from jax.experimental.pallas import tpu as pltpu
from jax.sharding import PartitionSpec as P

MESH = pl.DeviceIdType.MESH
F32 = jnp.float32
BF16 = jnp.bfloat16
EPSILON = 1e-05
N = 128
H = 128
ROWS, COLS = 32, 16
CHUNKS = 4
TOKENS = 256
OUT_LR, IN_LR, IN_SIDES, OUT_SIDES, IN_SUM, IN_SHARE = range(6)
OUT_TRI, IN_TRI, IN_BACK, OUT_BACK, OUT_SUM, OUT_SHARE = range(6, 12)
EXCHANGES = 12


def nn(a, b):
    return lax.dot_general(a, b, (((1,), (0,)), ((), ())), preferred_element_type=F32)


def nt(a, b):
    return lax.dot_general(a, b, (((1,), (1,)), ((), ())), preferred_element_type=F32)


def tn(a, b):
    return lax.dot_general(a, b, (((0,), (0,)), ((), ())), preferred_element_type=F32)


def token_rows(x):
    return [8 * hi + 4 * b + x for b in range(2) for hi in range(4)]


def at(x):
    return slice(128 * x, 128 * (x + 1))


def norm(v):
    shifted = v - jnp.mean(v, axis=0, keepdims=True)
    inv = lax.rsqrt(jnp.mean(shifted * shifted, axis=0, keepdims=True) + EPSILON)
    return shifted * inv, inv


def norm_grad(dy, y, inv):
    return inv * (
        dy - jnp.mean(dy, axis=0, keepdims=True) - y * jnp.mean(dy * y, axis=0, keepdims=True)
    )


def halves(a, b):
    low = lax.broadcasted_iota(jnp.int32, a.shape, 1) < 64
    moved = pltpu.roll(jnp.where(low, b, a), 64, 1)
    return jnp.where(low, a, moved), jnp.where(low, moved, b)


def interchange(v):
    group = lax.broadcasted_iota(jnp.int32, v[0].shape, 1) >> 4
    v = [v[0]] + [pltpu.roll(v[i], 16 * i, 1) for i in range(1, 8)]
    v = [v[-j % 8] for j in range(8)]
    for bit in (1, 2, 4):
        here = (group & bit) != 0
        v = [jnp.where(here, v[(j - bit) % 8], v[j]) for j in range(8)]
    return [v[0]] + [pltpu.roll(v[j], 128 - 16 * j, 1) for j in range(1, 8)]


def kernel(
    pair_in, cot_in, flags_in, wio_in, woo_in, wii_in, woi_in,
    upd_ref, pg_ref, gio_ref, goo_ref, gii_ref, goi_ref,
    send8, got8, send4, got4, share8, share4, wide, mats, tall, mask_ref,
    z_ref, y_ref, yinv_ref, n_ref, proj_ref, gate_ref, t_ref, tinv_ref, tn_ref, lifted_ref,
    sides_ref, res_ref, lg_ref, pgr_ref, wint_ref, woutt_ref,
    pair_ref, cot_ref, flags_ref, wio_ref, woo_ref, wii_ref, woi_ref,
    ssem, rsem, isem,
):
    loads = [
        pltpu.make_async_copy(src, dst, isem.at[n])
        for n, (src, dst) in enumerate((
            (pair_in, pair_ref), (wio_in, wio_ref), (flags_in, flags_ref), (woo_in, woo_ref),
            (cot_in, cot_ref), (wii_in, wii_ref), (woi_in, woi_ref),
        ))
    ]
    for load in loads:
        load.start()

    cols = lax.axis_size("col")
    row, col = lax.axis_index("row"), lax.axis_index("col")
    me = row * cols + col

    place_y, place_z, core = row // 2, col // 4, lax.rem(col, 2)
    place_x = lax.rem(col, 4) // 2 * 2 + lax.rem(row, 2)

    def turned(place, digit):
        return (place + (digit ^ (digit >> 1) ^ 2)) & 3

    others = [
        (turned(place_y, digit) * 2, core ^ last ^ 1) for digit in range(4) for last in range(2)
    ]

    def to_others(send):
        def some(step, among):
            z, x = turned(place_z, step >> 2), turned(place_x, step & 3)
            for y, c in among:
                send(y + (x & 1), z * 4 + (x >> 1) * 2 + c)

        @pl.loop(0, 15)
        def _(step):
            some(step, others)

        some(15, others[:-1])

    bar = pltpu.get_barrier_semaphore()

    to_others(
        lambda a, b: pl.semaphore_signal(bar, inc=1, device_id=(a, b), device_id_type=MESH)
    )

    def sent(k):
        return send8.at[k] if k < 6 else send4.at[k - 6]

    def got(k):
        return got8.at[k] if k < 6 else got4.at[k - 6]

    def start(k):
        source, target = sent(k), got(k)

        to_others(lambda a, b: pltpu.make_async_remote_copy(
            src_ref=source.at[a * cols + b], dst_ref=target.at[me], send_sem=ssem.at[k],
            recv_sem=rsem.at[k], device_id=(a, b), device_id_type=MESH,
        ).start())
        target[me] = source[me]

    def start_share(k):
        source, target = share8 if k < 6 else share4, got(k)

        to_others(lambda a, b: pltpu.make_async_remote_copy(
            src_ref=source, dst_ref=target.at[me], send_sem=ssem.at[k],
            recv_sem=rsem.at[k], device_id=(a, b), device_id_type=MESH,
        ).start())
        target[me] = source[...]

    def await_all(k, sem):
        part = got(k).at[pl.ds(0, N - 1)]
        pltpu.make_async_copy(part, part, sem.at[k]).wait()

    def put_pair(x, left, right):
        first, second = halves(left, right)
        wide[pl.ds(x, H, stride=8), :] = first
        wide[pl.ds(4 + x, H, stride=8), :] = second

    def put(x, value):
        wide[pl.ds(x, H, stride=4), :] = value

    def pack(k):
        if k < 6:
            sent(k)[...] = wide[...].reshape(N, 8, 128).astype(BF16)
            return
        for pair in range(N // 2):
            both = wide[8 * pair : 8 * pair + 8, :]
            sent(k)[2 * pair] = both[:4].astype(BF16)
            sent(k)[2 * pair + 1] = both[4:].astype(BF16)

    def unpack(k):
        if k < 6:
            wide[...] = got(k)[...].astype(F32).reshape(N * 8, 128)
            return
        for n in range(N):
            wide[4 * n : 4 * n + 4, :] = got(k)[n].astype(F32)

    def take_pair(x):
        return halves(wide[pl.ds(x, H, stride=8), :], wide[pl.ds(4 + x, H, stride=8), :])

    def take(x):
        return wide[pl.ds(x, H, stride=4), :]

    def spots(k, r, hi):
        if k < 6:
            return [
                (t, slice(r * 32 + ih * 8, r * 32 + ih * 8 + 8), at(hi))
                for t in range(2) for ih in range(4)
            ]
        return [
            (0, slice(r * 32 + ih * 8 + b * 4, r * 32 + ih * 8 + b * 4 + 4), at(hi))
            for b in range(2) for ih in range(4)
        ]

    def assemble(k):
        for r in range(8):
            for hi in range(2):
                v = interchange([got(k)[r * 16 + hi * 8 + lo].astype(F32) for lo in range(8)])
                for spot, part in zip(spots(k, r, hi), v):
                    tall[spot] = part

    def disperse(k):
        for r in range(8):
            for hi in range(2):
                v = interchange([tall[spot] for spot in spots(k, r, hi)])
                for lo in range(8):
                    sent(k)[r * 16 + hi * 8 + lo] = v[lo].astype(BF16)

    def set_in(w_in_ref, s):
        wint_ref[s] = w_in_ref[...].astype(F32).T.astype(BF16)

    def set_out(w_out_ref, s):
        woutt_ref[s] = w_out_ref[...].astype(F32).T.astype(BF16)

    def project(s, k, ready=lambda: None):
        for x in range(CHUNKS):
            y, inv = norm(z_ref[s, :, at(x)])
            y_ref[s, :, at(x)] = y
            yinv_ref[s, :, at(x)] = inv
            normed = y.astype(BF16)
            n_ref[s, :, at(x)] = normed
            mask = mask_ref[0:1, at(x)]
            p = nn(wint_ref[s], normed)
            proj_ref[s, :, at(x)] = p
            left = jax.nn.sigmoid(p[H : 2 * H]) * p[:H] * mask
            right = jax.nn.sigmoid(p[3 * H : 4 * H]) * p[2 * H : 3 * H] * mask
            put_pair(x, left, right)
        pack(k)
        ready()
        start(k)
        gate_ref[s] = jax.nn.sigmoid(proj_ref[s, 4 * H :, :])

    def multiply(s, k_in, k_out, outgoing):
        await_all(k_in, rsem)
        assemble(k_in)
        mats[s] = tall[...].astype(BF16)
        if outgoing:
            tall[0] = nt(mats[s, 0], mats[s, 1])
        else:
            tall[0] = tn(mats[s, 0], mats[s, 1])
        disperse(k_out)
        start(k_out)

    def lift(s, k, keep):
        await_all(k, rsem)
        unpack(k)
        for x in range(CHUNKS):
            y, inv = norm(take(x))
            t_ref[s, :, at(x)] = y
            tinv_ref[s, :, at(x)] = inv
            normed = y.astype(BF16)
            tn_ref[s, :, at(x)] = normed
            lifted = nn(woutt_ref[s], normed)
            lifted_ref[s, :, at(x)] = lifted
            keep(x, (z_ref[s, :, at(x)] + gate_ref[s, :, at(x)] * lifted).astype(BF16))

    def back(s, w_out_ref, k):
        for x in range(CHUNKS):
            dres = res_ref[s, :, at(x)]
            lift_grad = (gate_ref[s, :, at(x)] * dres).astype(BF16)
            lg_ref[s, :, at(x)] = lift_grad
            dy = nn(w_out_ref[...], lift_grad)
            tri_grad = norm_grad(dy, t_ref[s, :, at(x)], tinv_ref[s, :, at(x)])
            put(x, tri_grad)
        pack(k)
        start(k)
        for x in range(CHUNKS):
            gate = gate_ref[s, :, at(x)]
            pgr_ref[s, 4 * H :, at(x)] = (
                lifted_ref[s, :, at(x)] * res_ref[s, :, at(x)] * gate * (1.0 - gate)
            ).astype(BF16)

    def side_products(s, k_in, k_out, outgoing):
        await_all(k_in, rsem)
        assemble(k_in)
        grad = tall[0].astype(BF16)
        left, right = mats[s, 0], mats[s, 1]
        if outgoing:
            tall[0] = nn(grad, right)
            tall[1] = tn(grad, left)
        else:
            tall[0] = nt(right, grad)
            tall[1] = nn(left, grad)
        disperse(k_out)
        start(k_out)

    def side_grads(s, k):
        await_all(k, rsem)
        unpack(k)
        for x in range(CHUNKS):
            left_grad, right_grad = take_pair(x)
            mask = mask_ref[0:1, at(x)]
            p = proj_ref[s, :, at(x)]
            for side, grad in ((0, left_grad * mask), (2, right_grad * mask)):
                value = p[side * H : (side + 1) * H]
                sig = jax.nn.sigmoid(p[(side + 1) * H : (side + 2) * H])
                scaled = grad * sig
                pgr_ref[s, side * H : (side + 1) * H, at(x)] = scaled.astype(BF16)
                pgr_ref[s, (side + 1) * H : (side + 2) * H, at(x)] = (
                    scaled * value * (1.0 - sig)
                ).astype(BF16)

    def unproject(s, w_in_ref, keep):
        for x in range(CHUNKS):
            dres = res_ref[s, :, at(x)]
            dy = nn(w_in_ref[...], pgr_ref[s, :, at(x)])
            grad = norm_grad(dy, y_ref[s, :, at(x)], yinv_ref[s, :, at(x)])
            keep(x, (dres + grad).astype(BF16))

    def sum_early():
        w_in_grad = nt(n_ref[1], pgr_ref[1])
        for x in range(5):
            wide[pl.ds(x, H, stride=8), :] = w_in_grad[:, at(x)]
        wide[pl.ds(5, H, stride=8), :] = nt(tn_ref[1], lg_ref[1])
        wide[pl.ds(6, H, stride=8), :] = nt(tn_ref[0], lg_ref[0])
        wide[pl.ds(7, H, stride=8), :] = nt(n_ref[0], pgr_ref[0, 4 * H :, :])
        pack(IN_SUM)
        start(IN_SUM)

    def sum_late():
        w_in_grad = nt(n_ref[0], pgr_ref[0, : 4 * H, :])
        for x in range(4):
            put(x, w_in_grad[:, at(x)])
        pack(OUT_SUM)
        start(OUT_SUM)

    def share_sums(k_in, k_out):
        await_all(k_in, rsem)
        total = jnp.sum(got(k_in)[...].astype(F32), axis=0) * (1.0 / TOKENS)
        if k_in < 6:
            share8[...] = total.astype(BF16)
        else:
            share4[...] = total.astype(BF16)
        start_share(k_out)

    def give_early():
        await_all(IN_SHARE, rsem)
        unpack(IN_SHARE)
        for x in range(5):
            gii_ref[:, at(x)] = wide[pl.ds(x, H, stride=8), :]
        goi_ref[...] = wide[pl.ds(5, H, stride=8), :]
        goo_ref[...] = wide[pl.ds(6, H, stride=8), :]
        gio_ref[:, at(4)] = wide[pl.ds(7, H, stride=8), :]

    def give_late():
        await_all(OUT_SHARE, rsem)
        unpack(OUT_SHARE)
        for x in range(4):
            gio_ref[:, at(x)] = take(x)

    def write_tokens(ref, x, values):
        turned = values.astype(F32).T.astype(BF16)
        for m, i in enumerate(token_rows(x)):
            ref[i] = turned[16 * m : 16 * (m + 1)]

    def read_tokens(ref, x):
        return jnp.concatenate([ref[i] for i in token_rows(x)], axis=0).astype(F32).T

    for load in loads[:3]:
        load.wait()

    lane = lax.broadcasted_iota(jnp.int32, (TOKENS, 512), 1)
    token = lax.broadcasted_iota(jnp.int32, (TOKENS, 512), 0)
    own_row = row * ROWS + ((lane >> 4) & 3) * 8 + ((lane >> 6) & 1) * 4 + (lane >> 7)
    own_col = col * COLS + (lane & 15)
    flags = jnp.broadcast_to(flags_ref[...].astype(F32), (8, TOKENS)).astype(BF16)
    row_flags = nn(flags, jnp.where(token == own_row, 1.0, 0.0).astype(BF16))
    col_flags = nn(flags, jnp.where(token == own_col, 1.0, 0.0).astype(BF16))
    mask_ref[...] = row_flags * col_flags

    set_in(wio_ref, 0)
    for x in range(CHUNKS):
        z_ref[0, :, at(x)] = read_tokens(pair_ref, x)

    project(0, OUT_LR, lambda: pl.semaphore_wait(bar, N - 1))
    for load in loads[3:]:
        load.wait()
    set_out(woo_ref, 0)
    set_in(wii_ref, 1)
    set_out(woi_ref, 1)
    for x in range(CHUNKS):
        res_ref[1, :, at(x)] = read_tokens(cot_ref, x)
    multiply(0, OUT_LR, OUT_TRI, True)

    def keep_mid(x, mid):
        z_ref[1, :, at(x)] = mid.astype(F32)

    lift(0, OUT_TRI, keep_mid)
    project(1, IN_LR)
    multiply(1, IN_LR, IN_TRI, False)

    def keep_updated(x, updated):
        sides_ref[:, at(x)] = updated

    lift(1, IN_TRI, keep_updated)
    back(1, woi_ref, IN_BACK)
    for x in range(CHUNKS):
        write_tokens(upd_ref, x, sides_ref[:, at(x)])
    side_products(1, IN_BACK, IN_SIDES, False)

    def keep_mid_grad(x, grad):
        res_ref[0, :, at(x)] = grad.astype(F32)

    side_grads(1, IN_SIDES)
    unproject(1, wii_ref, keep_mid_grad)
    back(0, woo_ref, OUT_BACK)
    sum_early()
    side_products(0, OUT_BACK, OUT_SIDES, True)
    share_sums(IN_SUM, IN_SHARE)

    def keep_pair_grad(x, grad):
        sides_ref[:, at(x)] = grad

    side_grads(0, OUT_SIDES)
    sum_late()
    unproject(0, wio_ref, keep_pair_grad)
    for x in range(CHUNKS):
        write_tokens(pg_ref, x, sides_ref[:, at(x)])
    give_early()
    share_sums(OUT_SUM, OUT_SHARE)
    give_late()
    for k in range(EXCHANGES):
        await_all(k, ssem)


def deliver(*refs):
    copies = [
        pltpu.make_async_copy(refs[n], refs[6 + n], refs[12].at[n]) for n in (2, 4, 0, 1, 3, 5)
    ]
    for copy in copies:
        copy.start()
    for copy in copies:
        copy.wait()


def local(pair, cotangent, token_mask, out_in_proj, out_out_proj, in_in_proj, in_out_proj):
    tile = jax.ShapeDtypeStruct((ROWS, COLS, H), BF16)
    wide_grad = jax.ShapeDtypeStruct((H, 5 * H), F32)
    small_grad = jax.ShapeDtypeStruct((H, H), F32)
    vmem = pl.BlockSpec(memory_space=pltpu.VMEM)
    far = pl.BlockSpec(memory_space=pltpu.HBM)
    shapes = (tile, tile, wide_grad, small_grad, wide_grad, small_grad)
    results = pl.pallas_call(
        kernel,
        name="triangle_step",
        out_shape=tuple(pltpu.VMEM(s.shape, s.dtype) for s in shapes),
        in_specs=[far] * 7,
        out_specs=(vmem,) * 6,
        scratch_shapes=[
            pltpu.VMEM((6, N, 8, 128), BF16),
            pltpu.VMEM((6, N, 8, 128), BF16),
            pltpu.VMEM((6, N, 4, 128), BF16),
            pltpu.VMEM((6, N, 4, 128), BF16),
            pltpu.VMEM((8, 128), BF16),
            pltpu.VMEM((4, 128), BF16),
            pltpu.VMEM((N * 8, 128), F32),
            pltpu.VMEM((2, 2, TOKENS, TOKENS), BF16),
            pltpu.VMEM((2, TOKENS, TOKENS), F32),
            pltpu.VMEM((8, 512), F32),
            pltpu.VMEM((2, H, 512), F32),
            pltpu.VMEM((2, H, 512), F32),
            pltpu.VMEM((2, 1, 512), F32),
            pltpu.VMEM((2, H, 512), BF16),
            pltpu.VMEM((2, 5 * H, 512), F32),
            pltpu.VMEM((2, H, 512), F32),
            pltpu.VMEM((2, H, 512), F32),
            pltpu.VMEM((2, 1, 512), F32),
            pltpu.VMEM((2, H, 512), BF16),
            pltpu.VMEM((2, H, 512), F32),
            pltpu.VMEM((H, 512), BF16),
            pltpu.VMEM((2, H, 512), F32),
            pltpu.VMEM((2, H, 512), BF16),
            pltpu.VMEM((2, 5 * H, 512), BF16),
            pltpu.VMEM((2, 5 * H, H), BF16),
            pltpu.VMEM((2, H, H), BF16),
            pltpu.VMEM((ROWS, COLS, H), BF16),
            pltpu.VMEM((ROWS, COLS, H), BF16),
            pltpu.VMEM((1, TOKENS), jnp.int32),
            pltpu.VMEM((H, 5 * H), BF16),
            pltpu.VMEM((H, H), BF16),
            pltpu.VMEM((H, 5 * H), BF16),
            pltpu.VMEM((H, H), BF16),
            pltpu.SemaphoreType.DMA((EXCHANGES,)),
            pltpu.SemaphoreType.DMA((EXCHANGES,)),
            pltpu.SemaphoreType.DMA((7,)),
        ],
        compiler_params=pltpu.CompilerParams(
            collective_id=0, has_side_effects=True, vmem_limit_bytes=40 * 1024 * 1024
        ),
    )(*(
        pltpu.with_memory_space_constraint(array, pltpu.HBM)
        for array in (
            pair, cotangent, token_mask.reshape(1, TOKENS),
            out_in_proj, out_out_proj, in_in_proj, in_out_proj,
        )
    ))
    results = [pltpu.with_memory_space_constraint(r, pltpu.VMEM) for r in results]
    return pl.pallas_call(
        deliver,
        name="deliver",
        out_shape=shapes,
        in_specs=[vmem] * 6,
        out_specs=(far,) * 6,
        scratch_shapes=[pltpu.SemaphoreType.DMA((6,))],
    )(*results)


def solution(mesh):
    return jax.shard_map(
        local,
        mesh=mesh,
        in_specs=(P("row", "col", None), P("row", "col", None), P(), P(), P(), P(), P()),
        out_specs=(P("row", "col", None), P("row", "col", None), P(), P(), P(), P()),
        check_vma=False,
    )
```

```python
import jax
import jax.numpy as jnp
from jax import lax
from jax.experimental import pallas as pl
from jax.experimental.pallas import tpu as pltpu
from jax.sharding import PartitionSpec as P

MESH = pl.DeviceIdType.MESH
F32 = jnp.float32
BF16 = jnp.bfloat16
EPSILON = 1e-05
N = 128
H = 128
ROWS, COLS = 32, 16
CHUNKS = 4
TOKENS = 256
OUT_LR, IN_LR, IN_SIDES, OUT_SIDES, IN_SUM, IN_SHARE = range(6)
OUT_TRI, IN_TRI, IN_BACK, OUT_BACK, OUT_SUM, OUT_SHARE = range(6, 12)
EXCHANGES = 12


def nn(a, b):
    return lax.dot_general(a, b, (((1,), (0,)), ((), ())), preferred_element_type=F32)


def nt(a, b):
    return lax.dot_general(a, b, (((1,), (1,)), ((), ())), preferred_element_type=F32)


def tn(a, b):
    return lax.dot_general(a, b, (((0,), (0,)), ((), ())), preferred_element_type=F32)


def token_rows(x):
    return [8 * hi + 4 * b + x for b in range(2) for hi in range(4)]


def at(x):
    return slice(128 * x, 128 * (x + 1))


def norm(v):
    shifted = v - jnp.mean(v, axis=0, keepdims=True)
    inv = lax.rsqrt(jnp.mean(shifted * shifted, axis=0, keepdims=True) + EPSILON)
    return shifted * inv, inv


def norm_grad(dy, y, inv):
    return inv * (
        dy - jnp.mean(dy, axis=0, keepdims=True) - y * jnp.mean(dy * y, axis=0, keepdims=True)
    )


def halves(a, b):
    low = lax.broadcasted_iota(jnp.int32, a.shape, 1) < 64
    moved = pltpu.roll(jnp.where(low, b, a), 64, 1)
    return jnp.where(low, a, moved), jnp.where(low, moved, b)


def interchange(v):
    group = lax.broadcasted_iota(jnp.int32, v[0].shape, 1) >> 4
    v = [v[0]] + [pltpu.roll(v[i], 16 * i, 1) for i in range(1, 8)]
    v = [v[-j % 8] for j in range(8)]
    for bit in (1, 2, 4):
        here = (group & bit) != 0
        v = [jnp.where(here, v[(j - bit) % 8], v[j]) for j in range(8)]
    return [v[0]] + [pltpu.roll(v[j], 128 - 16 * j, 1) for j in range(1, 8)]


def kernel(
    pair_in, cot_in, flags_in, wio_in, woo_in, wii_in, woi_in,
    upd_ref, pg_ref, gio_ref, goo_ref, gii_ref, goi_ref,
    send8, got8, send4, got4, share8, share4, wide, mats, tall, mask_ref,
    z_ref, y_ref, yinv_ref, n_ref, proj_ref, gate_ref, t_ref, tinv_ref, tn_ref, lifted_ref,
    sides_ref, res_ref, lg_ref, pgr_ref, wint_ref, woutt_ref,
    pair_ref, cot_ref, flags_ref, wio_ref, woo_ref, wii_ref, woi_ref,
    ssem, rsem, isem,
):
    loads = [
        pltpu.make_async_copy(src, dst, isem.at[n])
        for n, (src, dst) in enumerate((
            (pair_in, pair_ref), (wio_in, wio_ref), (flags_in, flags_ref), (woo_in, woo_ref),
            (cot_in, cot_ref), (wii_in, wii_ref), (woi_in, woi_ref),
        ))
    ]
    for load in loads:
        load.start()

    cols = lax.axis_size("col")
    row, col = lax.axis_index("row"), lax.axis_index("col")
    me = row * cols + col

    place_y, place_z, core = row // 2, col // 4, lax.rem(col, 2)
    place_x = lax.rem(col, 4) // 2 * 2 + lax.rem(row, 2)

    def turned(place, digit):
        return (place + (digit ^ (digit >> 1) ^ 2) * (1 - 2 * core)) & 3

    others = [
        (turned(place_y, digit) * 2, core ^ last ^ 1) for digit in range(4) for last in range(2)
    ]

    def to_others(send):
        def some(z, x, among):
            for y, c in among:
                send(y + (x & 1), z * 4 + (x >> 1) * 2 + c)

        xs = [turned(place_x, digit) for digit in range(4)]

        @pl.loop(0, 3)
        def _(step):
            for x in xs:
                some(turned(place_z, step), x, others)

        for n, x in enumerate(xs):
            some(place_z, x, others if n < 3 else others[:-1])

    bar = pltpu.get_barrier_semaphore()

    to_others(
        lambda a, b: pl.semaphore_signal(bar, inc=1, device_id=(a, b), device_id_type=MESH)
    )

    def sent(k):
        return send8.at[k] if k < 6 else send4.at[k - 6]

    def got(k):
        return got8.at[k] if k < 6 else got4.at[k - 6]

    def start(k):
        source, target = sent(k), got(k)

        to_others(lambda a, b: pltpu.make_async_remote_copy(
            src_ref=source.at[a * cols + b], dst_ref=target.at[me], send_sem=ssem.at[k],
            recv_sem=rsem.at[k], device_id=(a, b), device_id_type=MESH,
        ).start())
        target[me] = source[me]

    def start_share(k):
        source, target = share8 if k < 6 else share4, got(k)

        to_others(lambda a, b: pltpu.make_async_remote_copy(
            src_ref=source, dst_ref=target.at[me], send_sem=ssem.at[k],
            recv_sem=rsem.at[k], device_id=(a, b), device_id_type=MESH,
        ).start())
        target[me] = source[...]

    def await_all(k, sem):
        part = got(k).at[pl.ds(0, N - 1)]
        pltpu.make_async_copy(part, part, sem.at[k]).wait()

    def put_pair(x, left, right):
        first, second = halves(left, right)
        wide[pl.ds(x, H, stride=8), :] = first
        wide[pl.ds(4 + x, H, stride=8), :] = second

    def put(x, value):
        wide[pl.ds(x, H, stride=4), :] = value

    def pack(k):
        if k < 6:
            sent(k)[...] = wide[...].reshape(N, 8, 128).astype(BF16)
            return
        for pair in range(N // 2):
            both = wide[8 * pair : 8 * pair + 8, :]
            sent(k)[2 * pair] = both[:4].astype(BF16)
            sent(k)[2 * pair + 1] = both[4:].astype(BF16)

    def unpack(k):
        if k < 6:
            wide[...] = got(k)[...].astype(F32).reshape(N * 8, 128)
            return
        for n in range(N):
            wide[4 * n : 4 * n + 4, :] = got(k)[n].astype(F32)

    def take_pair(x):
        return halves(wide[pl.ds(x, H, stride=8), :], wide[pl.ds(4 + x, H, stride=8), :])

    def take(x):
        return wide[pl.ds(x, H, stride=4), :]

    def spots(k, r, hi):
        if k < 6:
            return [
                (t, slice(r * 32 + ih * 8, r * 32 + ih * 8 + 8), at(hi))
                for t in range(2) for ih in range(4)
            ]
        return [
            (0, slice(r * 32 + ih * 8 + b * 4, r * 32 + ih * 8 + b * 4 + 4), at(hi))
            for b in range(2) for ih in range(4)
        ]

    def assemble(k):
        for r in range(8):
            for hi in range(2):
                v = interchange([got(k)[r * 16 + hi * 8 + lo].astype(F32) for lo in range(8)])
                for spot, part in zip(spots(k, r, hi), v):
                    tall[spot] = part

    def disperse(k):
        for r in range(8):
            for hi in range(2):
                v = interchange([tall[spot] for spot in spots(k, r, hi)])
                for lo in range(8):
                    sent(k)[r * 16 + hi * 8 + lo] = v[lo].astype(BF16)

    def set_in(w_in_ref, s):
        wint_ref[s] = w_in_ref[...].astype(F32).T.astype(BF16)

    def set_out(w_out_ref, s):
        woutt_ref[s] = w_out_ref[...].astype(F32).T.astype(BF16)

    def project(s, k, ready=lambda: None):
        for x in range(CHUNKS):
            y, inv = norm(z_ref[s, :, at(x)])
            y_ref[s, :, at(x)] = y
            yinv_ref[s, :, at(x)] = inv
            normed = y.astype(BF16)
            n_ref[s, :, at(x)] = normed
            mask = mask_ref[0:1, at(x)]
            p = nn(wint_ref[s], normed)
            proj_ref[s, :, at(x)] = p
            left = jax.nn.sigmoid(p[H : 2 * H]) * p[:H] * mask
            right = jax.nn.sigmoid(p[3 * H : 4 * H]) * p[2 * H : 3 * H] * mask
            put_pair(x, left, right)
        pack(k)
        ready()
        start(k)
        gate_ref[s] = jax.nn.sigmoid(proj_ref[s, 4 * H :, :])

    def multiply(s, k_in, k_out, outgoing):
        await_all(k_in, rsem)
        assemble(k_in)
        mats[s] = tall[...].astype(BF16)
        if outgoing:
            tall[0] = nt(mats[s, 0], mats[s, 1])
        else:
            tall[0] = tn(mats[s, 0], mats[s, 1])
        disperse(k_out)
        start(k_out)

    def lift(s, k, keep):
        await_all(k, rsem)
        unpack(k)
        for x in range(CHUNKS):
            y, inv = norm(take(x))
            t_ref[s, :, at(x)] = y
            tinv_ref[s, :, at(x)] = inv
            normed = y.astype(BF16)
            tn_ref[s, :, at(x)] = normed
            lifted = nn(woutt_ref[s], normed)
            lifted_ref[s, :, at(x)] = lifted
            keep(x, (z_ref[s, :, at(x)] + gate_ref[s, :, at(x)] * lifted).astype(BF16))

    def back(s, w_out_ref, k):
        for x in range(CHUNKS):
            dres = res_ref[s, :, at(x)]
            lift_grad = (gate_ref[s, :, at(x)] * dres).astype(BF16)
            lg_ref[s, :, at(x)] = lift_grad
            dy = nn(w_out_ref[...], lift_grad)
            tri_grad = norm_grad(dy, t_ref[s, :, at(x)], tinv_ref[s, :, at(x)])
            put(x, tri_grad)
        pack(k)
        start(k)
        for x in range(CHUNKS):
            gate = gate_ref[s, :, at(x)]
            pgr_ref[s, 4 * H :, at(x)] = (
                lifted_ref[s, :, at(x)] * res_ref[s, :, at(x)] * gate * (1.0 - gate)
            ).astype(BF16)

    def side_products(s, k_in, k_out, outgoing):
        await_all(k_in, rsem)
        assemble(k_in)
        grad = tall[0].astype(BF16)
        left, right = mats[s, 0], mats[s, 1]
        if outgoing:
            tall[0] = nn(grad, right)
            tall[1] = tn(grad, left)
        else:
            tall[0] = nt(right, grad)
            tall[1] = nn(left, grad)
        disperse(k_out)
        start(k_out)

    def side_grads(s, k):
        await_all(k, rsem)
        unpack(k)
        for x in range(CHUNKS):
            left_grad, right_grad = take_pair(x)
            mask = mask_ref[0:1, at(x)]
            p = proj_ref[s, :, at(x)]
            for side, grad in ((0, left_grad * mask), (2, right_grad * mask)):
                value = p[side * H : (side + 1) * H]
                sig = jax.nn.sigmoid(p[(side + 1) * H : (side + 2) * H])
                scaled = grad * sig
                pgr_ref[s, side * H : (side + 1) * H, at(x)] = scaled.astype(BF16)
                pgr_ref[s, (side + 1) * H : (side + 2) * H, at(x)] = (
                    scaled * value * (1.0 - sig)
                ).astype(BF16)

    def unproject(s, w_in_ref, keep):
        for x in range(CHUNKS):
            dres = res_ref[s, :, at(x)]
            dy = nn(w_in_ref[...], pgr_ref[s, :, at(x)])
            grad = norm_grad(dy, y_ref[s, :, at(x)], yinv_ref[s, :, at(x)])
            keep(x, (dres + grad).astype(BF16))

    def sum_early():
        w_in_grad = nt(n_ref[1], pgr_ref[1])
        for x in range(5):
            wide[pl.ds(x, H, stride=8), :] = w_in_grad[:, at(x)]
        wide[pl.ds(5, H, stride=8), :] = nt(tn_ref[1], lg_ref[1])
        wide[pl.ds(6, H, stride=8), :] = nt(tn_ref[0], lg_ref[0])
        wide[pl.ds(7, H, stride=8), :] = nt(n_ref[0], pgr_ref[0, 4 * H :, :])
        pack(IN_SUM)
        start(IN_SUM)

    def sum_late():
        w_in_grad = nt(n_ref[0], pgr_ref[0, : 4 * H, :])
        for x in range(4):
            put(x, w_in_grad[:, at(x)])
        pack(OUT_SUM)
        start(OUT_SUM)

    def share_sums(k_in, k_out):
        await_all(k_in, rsem)
        parts = [
            jnp.sum(got(k_in)[n : n + 16].astype(F32), axis=0) for n in range(0, N, 16)
        ]
        while len(parts) > 1:
            parts = [a + b for a, b in zip(parts[::2], parts[1::2])]
        total = parts[0] * (1.0 / TOKENS)
        if k_in < 6:
            share8[...] = total.astype(BF16)
        else:
            share4[...] = total.astype(BF16)
        start_share(k_out)

    def give_early():
        await_all(IN_SHARE, rsem)
        unpack(IN_SHARE)
        for x in range(5):
            gii_ref[:, at(x)] = wide[pl.ds(x, H, stride=8), :]
        goi_ref[...] = wide[pl.ds(5, H, stride=8), :]
        goo_ref[...] = wide[pl.ds(6, H, stride=8), :]
        gio_ref[:, at(4)] = wide[pl.ds(7, H, stride=8), :]

    def give_late():
        await_all(OUT_SHARE, rsem)
        unpack(OUT_SHARE)
        for x in range(4):
            gio_ref[:, at(x)] = take(x)

    def write_tokens(ref, x, values):
        turned = values.astype(F32).T.astype(BF16)
        for m, i in enumerate(token_rows(x)):
            ref[i] = turned[16 * m : 16 * (m + 1)]

    def read_tokens(ref, x):
        return jnp.concatenate([ref[i] for i in token_rows(x)], axis=0).astype(F32).T

    for load in loads[:3]:
        load.wait()

    lane = lax.broadcasted_iota(jnp.int32, (TOKENS, 512), 1)
    token = lax.broadcasted_iota(jnp.int32, (TOKENS, 512), 0)
    own_row = row * ROWS + ((lane >> 4) & 3) * 8 + ((lane >> 6) & 1) * 4 + (lane >> 7)
    own_col = col * COLS + (lane & 15)
    flags = jnp.broadcast_to(flags_ref[...].astype(F32), (8, TOKENS)).astype(BF16)
    row_flags = nn(flags, jnp.where(token == own_row, 1.0, 0.0).astype(BF16))
    col_flags = nn(flags, jnp.where(token == own_col, 1.0, 0.0).astype(BF16))
    mask_ref[...] = row_flags * col_flags

    set_in(wio_ref, 0)
    for x in range(CHUNKS):
        z_ref[0, :, at(x)] = read_tokens(pair_ref, x)

    project(0, OUT_LR, lambda: pl.semaphore_wait(bar, N - 1))
    for load in loads[3:]:
        load.wait()
    set_out(woo_ref, 0)
    set_in(wii_ref, 1)
    set_out(woi_ref, 1)
    for x in range(CHUNKS):
        res_ref[1, :, at(x)] = read_tokens(cot_ref, x)
    multiply(0, OUT_LR, OUT_TRI, True)

    def keep_mid(x, mid):
        z_ref[1, :, at(x)] = mid.astype(F32)

    lift(0, OUT_TRI, keep_mid)
    project(1, IN_LR)
    multiply(1, IN_LR, IN_TRI, False)

    def keep_updated(x, updated):
        sides_ref[:, at(x)] = updated

    lift(1, IN_TRI, keep_updated)
    back(1, woi_ref, IN_BACK)
    for x in range(CHUNKS):
        write_tokens(upd_ref, x, sides_ref[:, at(x)])
    side_products(1, IN_BACK, IN_SIDES, False)

    def keep_mid_grad(x, grad):
        res_ref[0, :, at(x)] = grad.astype(F32)

    side_grads(1, IN_SIDES)
    unproject(1, wii_ref, keep_mid_grad)
    back(0, woo_ref, OUT_BACK)
    sum_early()
    side_products(0, OUT_BACK, OUT_SIDES, True)
    share_sums(IN_SUM, IN_SHARE)

    def keep_pair_grad(x, grad):
        sides_ref[:, at(x)] = grad

    side_grads(0, OUT_SIDES)
    sum_late()
    unproject(0, wio_ref, keep_pair_grad)
    for x in range(CHUNKS):
        write_tokens(pg_ref, x, sides_ref[:, at(x)])
    give_early()
    share_sums(OUT_SUM, OUT_SHARE)
    give_late()
    for k in range(EXCHANGES):
        await_all(k, ssem)


def deliver(*refs):
    copies = [
        pltpu.make_async_copy(refs[n], refs[6 + n], refs[12].at[n]) for n in (2, 4, 0, 1, 3, 5)
    ]
    for copy in copies:
        copy.start()
    for copy in copies:
        copy.wait()


def local(pair, cotangent, token_mask, out_in_proj, out_out_proj, in_in_proj, in_out_proj):
    tile = jax.ShapeDtypeStruct((ROWS, COLS, H), BF16)
    wide_grad = jax.ShapeDtypeStruct((H, 5 * H), F32)
    small_grad = jax.ShapeDtypeStruct((H, H), F32)
    vmem = pl.BlockSpec(memory_space=pltpu.VMEM)
    far = pl.BlockSpec(memory_space=pltpu.HBM)
    shapes = (tile, tile, wide_grad, small_grad, wide_grad, small_grad)
    results = pl.pallas_call(
        kernel,
        name="triangle_step",
        out_shape=tuple(pltpu.VMEM(s.shape, s.dtype) for s in shapes),
        in_specs=[far] * 7,
        out_specs=(vmem,) * 6,
        scratch_shapes=[
            pltpu.VMEM((6, N, 8, 128), BF16),
            pltpu.VMEM((6, N, 8, 128), BF16),
            pltpu.VMEM((6, N, 4, 128), BF16),
            pltpu.VMEM((6, N, 4, 128), BF16),
            pltpu.VMEM((8, 128), BF16),
            pltpu.VMEM((4, 128), BF16),
            pltpu.VMEM((N * 8, 128), F32),
            pltpu.VMEM((2, 2, TOKENS, TOKENS), BF16),
            pltpu.VMEM((2, TOKENS, TOKENS), F32),
            pltpu.VMEM((8, 512), F32),
            pltpu.VMEM((2, H, 512), F32),
            pltpu.VMEM((2, H, 512), F32),
            pltpu.VMEM((2, 1, 512), F32),
            pltpu.VMEM((2, H, 512), BF16),
            pltpu.VMEM((2, 5 * H, 512), F32),
            pltpu.VMEM((2, H, 512), F32),
            pltpu.VMEM((2, H, 512), F32),
            pltpu.VMEM((2, 1, 512), F32),
            pltpu.VMEM((2, H, 512), BF16),
            pltpu.VMEM((2, H, 512), F32),
            pltpu.VMEM((H, 512), BF16),
            pltpu.VMEM((2, H, 512), F32),
            pltpu.VMEM((2, H, 512), BF16),
            pltpu.VMEM((2, 5 * H, 512), BF16),
            pltpu.VMEM((2, 5 * H, H), BF16),
            pltpu.VMEM((2, H, H), BF16),
            pltpu.VMEM((ROWS, COLS, H), BF16),
            pltpu.VMEM((ROWS, COLS, H), BF16),
            pltpu.VMEM((1, TOKENS), jnp.int32),
            pltpu.VMEM((H, 5 * H), BF16),
            pltpu.VMEM((H, H), BF16),
            pltpu.VMEM((H, 5 * H), BF16),
            pltpu.VMEM((H, H), BF16),
            pltpu.SemaphoreType.DMA((EXCHANGES,)),
            pltpu.SemaphoreType.DMA((EXCHANGES,)),
            pltpu.SemaphoreType.DMA((7,)),
        ],
        compiler_params=pltpu.CompilerParams(
            collective_id=0, has_side_effects=True, vmem_limit_bytes=40 * 1024 * 1024
        ),
    )(*(
        pltpu.with_memory_space_constraint(array, pltpu.HBM)
        for array in (
            pair, cotangent, token_mask.reshape(1, TOKENS),
            out_in_proj, out_out_proj, in_in_proj, in_out_proj,
        )
    ))
    results = [pltpu.with_memory_space_constraint(r, pltpu.VMEM) for r in results]
    return pl.pallas_call(
        deliver,
        name="deliver",
        out_shape=shapes,
        in_specs=[vmem] * 6,
        out_specs=(far,) * 6,
        scratch_shapes=[pltpu.SemaphoreType.DMA((6,))],
    )(*results)


def solution(mesh):
    return jax.shard_map(
        local,
        mesh=mesh,
        in_specs=(P("row", "col", None), P("row", "col", None), P(), P(), P(), P(), P()),
        out_specs=(P("row", "col", None), P("row", "col", None), P(), P(), P(), P()),
        check_vma=False,
    )
```

```python
import jax
import jax.numpy as jnp
from jax import lax
from jax.experimental import pallas as pl
from jax.experimental.pallas import tpu as pltpu
from jax.sharding import PartitionSpec as P

MESH = pl.DeviceIdType.MESH
F32 = jnp.float32
BF16 = jnp.bfloat16
EPSILON = 1e-05
N = 128
H = 128
ROWS, COLS = 32, 16
CHUNKS = 4
TOKENS = 256
OUT_LR, IN_LR, IN_SIDES, OUT_SIDES, IN_SUM, IN_SHARE = range(6)
OUT_TRI, IN_TRI, IN_BACK, OUT_BACK, OUT_SUM, OUT_SHARE = range(6, 12)
EXCHANGES = 12


def nn(a, b):
    return lax.dot_general(a, b, (((1,), (0,)), ((), ())), preferred_element_type=F32)


def nt(a, b):
    return lax.dot_general(a, b, (((1,), (1,)), ((), ())), preferred_element_type=F32)


def tn(a, b):
    return lax.dot_general(a, b, (((0,), (0,)), ((), ())), preferred_element_type=F32)


def token_rows(x):
    return [8 * hi + 4 * b + x for b in range(2) for hi in range(4)]


def at(x):
    return slice(128 * x, 128 * (x + 1))


def norm(v):
    shifted = v - jnp.mean(v, axis=0, keepdims=True)
    inv = lax.rsqrt(jnp.mean(shifted * shifted, axis=0, keepdims=True) + EPSILON)
    return shifted * inv, inv


def norm_grad(dy, y, inv):
    return inv * (
        dy - jnp.mean(dy, axis=0, keepdims=True) - y * jnp.mean(dy * y, axis=0, keepdims=True)
    )


def halves(a, b):
    low = lax.broadcasted_iota(jnp.int32, a.shape, 1) < 64
    moved = pltpu.roll(jnp.where(low, b, a), 64, 1)
    return jnp.where(low, a, moved), jnp.where(low, moved, b)


def interchange(v):
    group = lax.broadcasted_iota(jnp.int32, v[0].shape, 1) >> 4
    v = [v[0]] + [pltpu.roll(v[i], 16 * i, 1) for i in range(1, 8)]
    v = [v[-j % 8] for j in range(8)]
    for bit in (1, 2, 4):
        here = (group & bit) != 0
        v = [jnp.where(here, v[(j - bit) % 8], v[j]) for j in range(8)]
    return [v[0]] + [pltpu.roll(v[j], 128 - 16 * j, 1) for j in range(1, 8)]


def kernel(
    pair_in, cot_in, flags_in, wio_in, woo_in, wii_in, woi_in,
    upd_ref, pg_ref, gio_ref, goo_ref, gii_ref, goi_ref,
    send8, got8, send4, got4, share8, share4, wide, mats, tall, mask_ref,
    z_ref, y_ref, yinv_ref, n_ref, proj_ref, gate_ref, t_ref, tinv_ref, tn_ref, lifted_ref,
    sides_ref, res_ref, lg_ref, pgr_ref, wint_ref, woutt_ref,
    pair_ref, cot_ref, flags_ref, wio_ref, woo_ref, wii_ref, woi_ref,
    ssem, rsem, isem,
):
    loads = [
        pltpu.make_async_copy(src, dst, isem.at[n])
        for n, (src, dst) in enumerate((
            (pair_in, pair_ref), (wio_in, wio_ref), (flags_in, flags_ref), (woo_in, woo_ref),
            (cot_in, cot_ref), (wii_in, wii_ref), (woi_in, woi_ref),
        ))
    ]
    for load in loads:
        load.start()

    cols = lax.axis_size("col")
    row, col = lax.axis_index("row"), lax.axis_index("col")
    me = row * cols + col

    place_y, place_z, core = row // 2, col // 4, lax.rem(col, 2)
    place_x = lax.rem(col, 4) // 2 * 2 + lax.rem(row, 2)

    def turned(place, digit):
        return (place + (digit ^ (digit >> 1) ^ 2) * (1 - 2 * core)) & 3

    others = [
        (turned(place_y, digit) * 2, core ^ last ^ 1) for digit in range(4) for last in range(2)
    ]

    def to_others(send):
        def some(z, x, among):
            for y, c in among:
                send(y + (x & 1), z * 4 + (x >> 1) * 2 + c)

        xs = [turned(place_x, digit) for digit in range(4)]

        @pl.loop(0, 3)
        def _(step):
            for x in xs:
                some(turned(place_z, step), x, others)

        for n, x in enumerate(xs):
            some(place_z, x, others if n < 3 else others[:-1])

    bar = pltpu.get_barrier_semaphore()

    to_others(
        lambda a, b: pl.semaphore_signal(bar, inc=1, device_id=(a, b), device_id_type=MESH)
    )

    def sent(k):
        return send8.at[k] if k < 6 else send4.at[k - 6]

    def got(k):
        return got8.at[k] if k < 6 else got4.at[k - 6]

    def start(k):
        source, target = sent(k), got(k)

        to_others(lambda a, b: pltpu.make_async_remote_copy(
            src_ref=source.at[a * cols + b], dst_ref=target.at[me], send_sem=ssem.at[k],
            recv_sem=rsem.at[k], device_id=(a, b), device_id_type=MESH,
        ).start())
        target[me] = source[me]

    def start_share(k):
        source, target = share8 if k < 6 else share4, got(k)

        to_others(lambda a, b: pltpu.make_async_remote_copy(
            src_ref=source, dst_ref=target.at[me], send_sem=ssem.at[k],
            recv_sem=rsem.at[k], device_id=(a, b), device_id_type=MESH,
        ).start())
        target[me] = source[...]

    def await_all(k, sem):
        part = got(k).at[pl.ds(0, N - 1)]
        pltpu.make_async_copy(part, part, sem.at[k]).wait()

    def put_pair(x, left, right):
        first, second = halves(left, right)
        wide[pl.ds(x, H, stride=8), :] = first
        wide[pl.ds(4 + x, H, stride=8), :] = second

    def put(x, value):
        wide[pl.ds(x, H, stride=4), :] = value

    def pack(k):
        if k < 6:
            sent(k)[...] = wide[...].reshape(N, 8, 128).astype(BF16)
            return
        for pair in range(N // 2):
            both = wide[8 * pair : 8 * pair + 8, :]
            sent(k)[2 * pair] = both[:4].astype(BF16)
            sent(k)[2 * pair + 1] = both[4:].astype(BF16)

    def unpack(k):
        if k < 6:
            wide[...] = got(k)[...].astype(F32).reshape(N * 8, 128)
            return
        for n in range(N):
            wide[4 * n : 4 * n + 4, :] = got(k)[n].astype(F32)

    def take_pair(x):
        return halves(wide[pl.ds(x, H, stride=8), :], wide[pl.ds(4 + x, H, stride=8), :])

    def take(x):
        return wide[pl.ds(x, H, stride=4), :]

    def spots(k, r, hi):
        if k < 6:
            return [
                (t, slice(r * 32 + ih * 8, r * 32 + ih * 8 + 8), at(hi))
                for t in range(2) for ih in range(4)
            ]
        return [
            (0, slice(r * 32 + ih * 8 + b * 4, r * 32 + ih * 8 + b * 4 + 4), at(hi))
            for b in range(2) for ih in range(4)
        ]

    def assemble(k):
        for r in range(8):
            for hi in range(2):
                v = interchange([got(k)[r * 16 + hi * 8 + lo].astype(F32) for lo in range(8)])
                for spot, part in zip(spots(k, r, hi), v):
                    tall[spot] = part

    def disperse(k):
        for r in range(8):
            for hi in range(2):
                v = interchange([tall[spot] for spot in spots(k, r, hi)])
                for lo in range(8):
                    sent(k)[r * 16 + hi * 8 + lo] = v[lo].astype(BF16)

    def set_in(w_in_ref, s):
        wint_ref[s] = w_in_ref[...].astype(F32).T.astype(BF16)

    def set_out(w_out_ref, s):
        woutt_ref[s] = w_out_ref[...].astype(F32).T.astype(BF16)

    def project(s, k, ready=lambda: None):
        for x in range(CHUNKS):
            y, inv = norm(z_ref[s, :, at(x)])
            y_ref[s, :, at(x)] = y
            yinv_ref[s, :, at(x)] = inv
            normed = y.astype(BF16)
            n_ref[s, :, at(x)] = normed
            mask = mask_ref[0:1, at(x)]
            p = nn(wint_ref[s], normed)
            proj_ref[s, :, at(x)] = p
            left_sig, right_sig = jax.nn.sigmoid(p[H : 2 * H]), jax.nn.sigmoid(p[3 * H : 4 * H])
            proj_ref[s, H : 2 * H, at(x)] = left_sig
            proj_ref[s, 3 * H : 4 * H, at(x)] = right_sig
            left = left_sig * p[:H] * mask
            right = right_sig * p[2 * H : 3 * H] * mask
            put_pair(x, left, right)
        pack(k)
        ready()
        start(k)
        gate_ref[s] = jax.nn.sigmoid(proj_ref[s, 4 * H :, :])

    def multiply(s, k_in, k_out, outgoing):
        await_all(k_in, rsem)
        assemble(k_in)
        mats[s] = tall[...].astype(BF16)
        if outgoing:
            tall[0] = nt(mats[s, 0], mats[s, 1])
        else:
            tall[0] = tn(mats[s, 0], mats[s, 1])
        disperse(k_out)
        start(k_out)

    def lift(s, k, keep):
        await_all(k, rsem)
        unpack(k)
        for x in range(CHUNKS):
            y, inv = norm(take(x))
            t_ref[s, :, at(x)] = y
            tinv_ref[s, :, at(x)] = inv
            normed = y.astype(BF16)
            tn_ref[s, :, at(x)] = normed
            lifted = nn(woutt_ref[s], normed)
            lifted_ref[s, :, at(x)] = lifted
            keep(x, (z_ref[s, :, at(x)] + gate_ref[s, :, at(x)] * lifted).astype(BF16))

    def back(s, w_out_ref, k):
        for x in range(CHUNKS):
            dres = res_ref[s, :, at(x)]
            lift_grad = (gate_ref[s, :, at(x)] * dres).astype(BF16)
            lg_ref[s, :, at(x)] = lift_grad
            dy = nn(w_out_ref[...], lift_grad)
            tri_grad = norm_grad(dy, t_ref[s, :, at(x)], tinv_ref[s, :, at(x)])
            put(x, tri_grad)
        pack(k)
        start(k)
        for x in range(CHUNKS):
            gate = gate_ref[s, :, at(x)]
            pgr_ref[s, 4 * H :, at(x)] = (
                lifted_ref[s, :, at(x)] * res_ref[s, :, at(x)] * gate * (1.0 - gate)
            ).astype(BF16)

    def side_products(s, k_in, k_out, outgoing):
        await_all(k_in, rsem)
        assemble(k_in)
        grad = tall[0].astype(BF16)
        left, right = mats[s, 0], mats[s, 1]
        if outgoing:
            tall[0] = nn(grad, right)
            tall[1] = tn(grad, left)
        else:
            tall[0] = nt(right, grad)
            tall[1] = nn(left, grad)
        disperse(k_out)
        start(k_out)

    def side_grads(s, k):
        await_all(k, rsem)
        unpack(k)
        for x in range(CHUNKS):
            left_grad, right_grad = take_pair(x)
            mask = mask_ref[0:1, at(x)]
            p = proj_ref[s, :, at(x)]
            for side, grad in ((0, left_grad * mask), (2, right_grad * mask)):
                value = p[side * H : (side + 1) * H]
                sig = p[(side + 1) * H : (side + 2) * H]
                scaled = grad * sig
                pgr_ref[s, side * H : (side + 1) * H, at(x)] = scaled.astype(BF16)
                pgr_ref[s, (side + 1) * H : (side + 2) * H, at(x)] = (
                    scaled * value * (1.0 - sig)
                ).astype(BF16)

    def unproject(s, w_in_ref, keep):
        for x in range(CHUNKS):
            dres = res_ref[s, :, at(x)]
            dy = nn(w_in_ref[...], pgr_ref[s, :, at(x)])
            grad = norm_grad(dy, y_ref[s, :, at(x)], yinv_ref[s, :, at(x)])
            keep(x, (dres + grad).astype(BF16))

    def sum_early():
        w_in_grad = nt(n_ref[1], pgr_ref[1])
        for x in range(5):
            wide[pl.ds(x, H, stride=8), :] = w_in_grad[:, at(x)]
        wide[pl.ds(5, H, stride=8), :] = nt(tn_ref[1], lg_ref[1])
        wide[pl.ds(6, H, stride=8), :] = nt(tn_ref[0], lg_ref[0])
        wide[pl.ds(7, H, stride=8), :] = nt(n_ref[0], pgr_ref[0, 4 * H :, :])
        pack(IN_SUM)
        start(IN_SUM)

    def sum_late():
        w_in_grad = nt(n_ref[0], pgr_ref[0, : 4 * H, :])
        for x in range(4):
            put(x, w_in_grad[:, at(x)])
        pack(OUT_SUM)
        start(OUT_SUM)

    def share_sums(k_in, k_out):
        await_all(k_in, rsem)
        parts = [
            jnp.sum(got(k_in)[n : n + 16].astype(F32), axis=0) for n in range(0, N, 16)
        ]
        while len(parts) > 1:
            parts = [a + b for a, b in zip(parts[::2], parts[1::2])]
        total = parts[0] * (1.0 / TOKENS)
        if k_in < 6:
            share8[...] = total.astype(BF16)
        else:
            share4[...] = total.astype(BF16)
        start_share(k_out)

    def give_early():
        await_all(IN_SHARE, rsem)
        unpack(IN_SHARE)
        for x in range(5):
            gii_ref[:, at(x)] = wide[pl.ds(x, H, stride=8), :]
        goi_ref[...] = wide[pl.ds(5, H, stride=8), :]
        goo_ref[...] = wide[pl.ds(6, H, stride=8), :]
        gio_ref[:, at(4)] = wide[pl.ds(7, H, stride=8), :]

    def give_late():
        await_all(OUT_SHARE, rsem)
        unpack(OUT_SHARE)
        for x in range(4):
            gio_ref[:, at(x)] = take(x)

    def write_tokens(ref, x, values):
        turned = values.astype(F32).T.astype(BF16)
        for m, i in enumerate(token_rows(x)):
            ref[i] = turned[16 * m : 16 * (m + 1)]

    def read_tokens(ref, x):
        return jnp.concatenate([ref[i] for i in token_rows(x)], axis=0).astype(F32).T

    for load in loads[:3]:
        load.wait()

    lane = lax.broadcasted_iota(jnp.int32, (TOKENS, 512), 1)
    token = lax.broadcasted_iota(jnp.int32, (TOKENS, 512), 0)
    own_row = row * ROWS + ((lane >> 4) & 3) * 8 + ((lane >> 6) & 1) * 4 + (lane >> 7)
    own_col = col * COLS + (lane & 15)
    flags = jnp.broadcast_to(flags_ref[...].astype(F32), (8, TOKENS)).astype(BF16)
    row_flags = nn(flags, jnp.where(token == own_row, 1.0, 0.0).astype(BF16))
    col_flags = nn(flags, jnp.where(token == own_col, 1.0, 0.0).astype(BF16))
    mask_ref[...] = row_flags * col_flags

    set_in(wio_ref, 0)
    for x in range(CHUNKS):
        z_ref[0, :, at(x)] = read_tokens(pair_ref, x)

    project(0, OUT_LR, lambda: pl.semaphore_wait(bar, N - 1))
    for load in loads[3:]:
        load.wait()
    set_out(woo_ref, 0)
    set_in(wii_ref, 1)
    set_out(woi_ref, 1)
    for x in range(CHUNKS):
        res_ref[1, :, at(x)] = read_tokens(cot_ref, x)
    multiply(0, OUT_LR, OUT_TRI, True)

    def keep_mid(x, mid):
        z_ref[1, :, at(x)] = mid.astype(F32)

    lift(0, OUT_TRI, keep_mid)
    project(1, IN_LR)
    multiply(1, IN_LR, IN_TRI, False)

    def keep_updated(x, updated):
        sides_ref[:, at(x)] = updated

    lift(1, IN_TRI, keep_updated)
    back(1, woi_ref, IN_BACK)
    for x in range(CHUNKS):
        write_tokens(upd_ref, x, sides_ref[:, at(x)])
    side_products(1, IN_BACK, IN_SIDES, False)

    def keep_mid_grad(x, grad):
        res_ref[0, :, at(x)] = grad.astype(F32)

    side_grads(1, IN_SIDES)
    unproject(1, wii_ref, keep_mid_grad)
    back(0, woo_ref, OUT_BACK)
    sum_early()
    side_products(0, OUT_BACK, OUT_SIDES, True)
    share_sums(IN_SUM, IN_SHARE)

    def keep_pair_grad(x, grad):
        sides_ref[:, at(x)] = grad

    side_grads(0, OUT_SIDES)
    sum_late()
    unproject(0, wio_ref, keep_pair_grad)
    for x in range(CHUNKS):
        write_tokens(pg_ref, x, sides_ref[:, at(x)])
    give_early()
    share_sums(OUT_SUM, OUT_SHARE)
    give_late()
    for k in range(EXCHANGES):
        await_all(k, ssem)


def deliver(*refs):
    copies = [
        pltpu.make_async_copy(refs[n], refs[6 + n], refs[12].at[n]) for n in (2, 4, 0, 1, 3, 5)
    ]
    for copy in copies:
        copy.start()
    for copy in copies:
        copy.wait()


def local(pair, cotangent, token_mask, out_in_proj, out_out_proj, in_in_proj, in_out_proj):
    tile = jax.ShapeDtypeStruct((ROWS, COLS, H), BF16)
    wide_grad = jax.ShapeDtypeStruct((H, 5 * H), F32)
    small_grad = jax.ShapeDtypeStruct((H, H), F32)
    vmem = pl.BlockSpec(memory_space=pltpu.VMEM)
    far = pl.BlockSpec(memory_space=pltpu.HBM)
    shapes = (tile, tile, wide_grad, small_grad, wide_grad, small_grad)
    results = pl.pallas_call(
        kernel,
        name="triangle_step",
        out_shape=tuple(pltpu.VMEM(s.shape, s.dtype) for s in shapes),
        in_specs=[far] * 7,
        out_specs=(vmem,) * 6,
        scratch_shapes=[
            pltpu.VMEM((6, N, 8, 128), BF16),
            pltpu.VMEM((6, N, 8, 128), BF16),
            pltpu.VMEM((6, N, 4, 128), BF16),
            pltpu.VMEM((6, N, 4, 128), BF16),
            pltpu.VMEM((8, 128), BF16),
            pltpu.VMEM((4, 128), BF16),
            pltpu.VMEM((N * 8, 128), F32),
            pltpu.VMEM((2, 2, TOKENS, TOKENS), BF16),
            pltpu.VMEM((2, TOKENS, TOKENS), F32),
            pltpu.VMEM((8, 512), F32),
            pltpu.VMEM((2, H, 512), F32),
            pltpu.VMEM((2, H, 512), F32),
            pltpu.VMEM((2, 1, 512), F32),
            pltpu.VMEM((2, H, 512), BF16),
            pltpu.VMEM((2, 5 * H, 512), F32),
            pltpu.VMEM((2, H, 512), F32),
            pltpu.VMEM((2, H, 512), F32),
            pltpu.VMEM((2, 1, 512), F32),
            pltpu.VMEM((2, H, 512), BF16),
            pltpu.VMEM((2, H, 512), F32),
            pltpu.VMEM((H, 512), BF16),
            pltpu.VMEM((2, H, 512), F32),
            pltpu.VMEM((2, H, 512), BF16),
            pltpu.VMEM((2, 5 * H, 512), BF16),
            pltpu.VMEM((2, 5 * H, H), BF16),
            pltpu.VMEM((2, H, H), BF16),
            pltpu.VMEM((ROWS, COLS, H), BF16),
            pltpu.VMEM((ROWS, COLS, H), BF16),
            pltpu.VMEM((1, TOKENS), jnp.int32),
            pltpu.VMEM((H, 5 * H), BF16),
            pltpu.VMEM((H, H), BF16),
            pltpu.VMEM((H, 5 * H), BF16),
            pltpu.VMEM((H, H), BF16),
            pltpu.SemaphoreType.DMA((EXCHANGES,)),
            pltpu.SemaphoreType.DMA((EXCHANGES,)),
            pltpu.SemaphoreType.DMA((7,)),
        ],
        compiler_params=pltpu.CompilerParams(
            collective_id=0, has_side_effects=True, vmem_limit_bytes=40 * 1024 * 1024
        ),
    )(*(
        pltpu.with_memory_space_constraint(array, pltpu.HBM)
        for array in (
            pair, cotangent, token_mask.reshape(1, TOKENS),
            out_in_proj, out_out_proj, in_in_proj, in_out_proj,
        )
    ))
    results = [pltpu.with_memory_space_constraint(r, pltpu.VMEM) for r in results]
    return pl.pallas_call(
        deliver,
        name="deliver",
        out_shape=shapes,
        in_specs=[vmem] * 6,
        out_specs=(far,) * 6,
        scratch_shapes=[pltpu.SemaphoreType.DMA((6,))],
    )(*results)


def solution(mesh):
    return jax.shard_map(
        local,
        mesh=mesh,
        in_specs=(P("row", "col", None), P("row", "col", None), P(), P(), P(), P(), P()),
        out_specs=(P("row", "col", None), P("row", "col", None), P(), P(), P(), P()),
        check_vma=False,
    )
```
